1024 devices in a mesh: space: 32 (over y, z_hi, core), vel: 32 (over z_lo, x).
Axes of the slice: x: 4, y: 4, z: 32 (z_hi: 4, z_lo: 8; z = z_hi * 8 + z_lo), core: 2. Of those that a mesh axis runs over, the one named last changes fastest.
Arguments:
- phase_density_field: float32 [5, 32, 1024, 1024], P(None, 'vel', 'space'), may hold values from 0.2 to 2.8, as said below
- fourier_scattering_table: float32 [3, 32, 1024], replicated, may hold values from -4 to 4
- odd_stiffness_factor: float32 [5], replicated, may hold values from 0.5 to 8
- electron_bgk_frequency_dt: float32 [2], replicated, may hold values from 0.5 to 4
- electron_kinetic_heat_level: float32 [2], replicated, may hold values from 8 to 24
Outputs:
- next_distribution: float32 [5, 32, 1024, 1024], P(None, 'vel', 'space')
The draws below stay inside these ranges and needn't reach their ends.
Inputs may be any that keep to these rules, and one draw needn't show every extreme that they name: `phase_density_field`: every entry is positive.
All inputs are finite; a program needn't handle non-finite values.
Results may differ from the reference program's by a relative error of at most 0.0001.
Values sent between devices are 32-bit elements; how exact they have to be, the bound alone decides.
A program may use at most 32 MiB of HBM per device.

```python
import math
import jax
import jax.numpy as jnp
from jax import lax

NVX = 32
NVY = 32
NVZ = 32
HEAVY = 3
ELECTRON_GROUPS = 2
SPECIES = 5
PAIRS = 1
KERNELS = 3
NX = 1024


def draw_phase_density_field(key, part):
    key_rough = jax.random.fold_in(key, 0)
    indices = jnp.arange(NVX, dtype=jnp.float32)
    slopes = (2.0 * indices - (NVX - 1)) / (NVX - 1)
    full_shape = (SPECIES, NVX, NX, NVY * NVZ)
    ramping = 1.0 + 0.5 * slopes
    roughness = 1.0 + 0.4 * jnp.clip(jax.random.normal(key_rough, full_shape, jnp.float32), -1.0, 1.0)
    return ramping[None, :, None, None] * roughness


def scatter_about(key, shape, scale, limit, held_as=jnp.bfloat16):
    array = jax.random.normal(key, shape, jnp.float32) * scale
    return jnp.minimum(jnp.maximum(array, -limit), limit).astype(held_as)


def setup_inputs(seed: int = 0) -> dict:
    keys = jax.random.split(jax.random.key(seed), 6)
    phase_density_field = draw_phase_density_field(jax.random.fold_in(keys[5], 71), 0)
    fourier_scattering_table = scatter_about(keys[1], (KERNELS, NVX, NVY * NVZ), 0.7, 4.0, jnp.float32)
    odd_stiffness_factor = jnp.clip(jnp.exp(jax.random.uniform(keys[2], (SPECIES,), jnp.float32, math.log(0.5), math.log(8.0))), 0.5, 8.0)
    electron_bgk_frequency_dt = jnp.clip(jnp.exp(jax.random.uniform(keys[3], (ELECTRON_GROUPS,), jnp.float32, math.log(0.5), math.log(4.0))), 0.5, 4.0)
    electron_kinetic_heat_level = jnp.clip(jnp.exp(jax.random.uniform(keys[4], (ELECTRON_GROUPS,), jnp.float32, math.log(8.0), math.log(24.0))), 8.0, 24.0)
    return {"phase_density_field": phase_density_field, "fourier_scattering_table": fourier_scattering_table, "odd_stiffness_factor": odd_stiffness_factor, "electron_bgk_frequency_dt": electron_bgk_frequency_dt, "electron_kinetic_heat_level": electron_kinetic_heat_level}


CFL_NUMBER = 0.2
VELOCITY_STEP = 0.375
COLLIDE_SCALE = 0.25


def velocity_values(indices, extent):
    return (indices.astype(jnp.float32) - (extent - 1) / 2.0) * VELOCITY_STEP


def plane_speed(indices, extent):
    return CFL_NUMBER * (2 * indices - (extent - 1)).astype(jnp.float32) / (extent - 1)


def reorder(fields):
    half = fields.shape[1] // 2
    return jnp.concatenate([fields[:, :half], jnp.flip(fields[:, half:], axis=1)], axis=1)


def reference(phase_density_field, fourier_scattering_table, odd_stiffness_factor, electron_bgk_frequency_dt, electron_kinetic_heat_level):
    natural = reorder(phase_density_field)
    speeds = plane_speed(jnp.arange(NVX, dtype=jnp.int32), NVX)[:, None, None]

    def advance_one(inputs):
        fields, relax_one = inputs
        mirror = jnp.flip(fields, axis=(0, 2))
        even_part = 0.5 * (fields + mirror)
        odd_part = 0.5 * (fields - mirror)
        even_diff = 0.5 * (jnp.roll(even_part, -1, axis=1) - jnp.roll(even_part, 1, axis=1))
        odd_diff = 0.5 * (jnp.roll(odd_part, -1, axis=1) - jnp.roll(odd_part, 1, axis=1))
        even_new = even_part - speeds * odd_diff
        odd_new = (odd_part - speeds * even_diff) / (1.0 + relax_one)
        return even_new + odd_new

    advanced = lax.map(advance_one, (natural, odd_stiffness_factor))

    def collide_one(fields):
        cube = fields.reshape(NVX, NX, NVY, NVZ)
        spectrum = jnp.fft.fftn(cube, axes=(0, 2, 3))

        def invert(kernel_index):
            kernel = fourier_scattering_table[kernel_index].reshape(NVX, 1, NVY, NVZ)
            inverse = jnp.fft.ifftn(kernel * spectrum, axes=(0, 2, 3))
            return jnp.real(inverse).reshape(NVX, NX, NVY * NVZ)

        gain_sum = invert(0) * invert(1)
        for pairing in range(1, PAIRS):
            gain_sum = gain_sum + invert(2 * pairing) * invert(2 * pairing + 1)
        loss_term = fields * invert(2 * PAIRS)
        return fields + COLLIDE_SCALE * (gain_sum - loss_term)

    heavy_next = lax.map(collide_one, advanced[:HEAVY])

    light_portion = advanced[HEAVY:]
    along_first = velocity_values(jnp.arange(NVX, dtype=jnp.int32), NVX)
    grid_second = velocity_values(jnp.arange(NVY, dtype=jnp.int32), NVY)
    grid_third = velocity_values(jnp.arange(NVZ, dtype=jnp.int32), NVZ)
    along_second = jnp.repeat(grid_second, NVZ)
    along_third = jnp.tile(grid_third, NVY)
    density = jnp.sum(light_portion, axis=(1, 3))
    drift_first = jnp.sum(light_portion * along_first[None, :, None, None], axis=(1, 3)) / density
    drift_second = jnp.sum(light_portion * along_second, axis=(1, 3)) / density
    drift_third = jnp.sum(light_portion * along_third, axis=(1, 3)) / density
    equilibrium_heat_level = electron_kinetic_heat_level[:, None, None]

    def profile(values, drift):
        offset_counts_per_row = values[None, None, :] - drift[:, :, None]
        integration_coefficient = jnp.exp(-(offset_counts_per_row * offset_counts_per_row) / (2.0 * equilibrium_heat_level))
        return integration_coefficient / jnp.sum(integration_coefficient, axis=2, keepdims=True)

    profile_first = profile(along_first, drift_first)
    profile_rest = (profile(grid_second, drift_second)[:, :, :, None] * profile(grid_third, drift_third)[:, :, None, :]).reshape(ELECTRON_GROUPS, NX, NVY * NVZ)
    maxwell = density[:, None, :, None] * jnp.transpose(profile_first, (0, 2, 1))[:, :, :, None] * profile_rest[:, None, :, :]
    rates = electron_bgk_frequency_dt[:, None, None, None]
    light_next = (light_portion + rates * maxwell) / (1.0 + rates)
    return reorder(jnp.concatenate([heavy_next, light_next], axis=0))
```

```python
import math

import jax
import jax.numpy as jnp
from jax import lax
from jax.sharding import PartitionSpec as P

NVX = 32
NVY = 32
NVZ = 32
PAIRS = 1


CFL_NUMBER = 0.2
VELOCITY_STEP = 0.375
COLLIDE_SCALE = 0.25


def extended(x, sides, width):
    for axis, dim in sides:
        devices, length = (lax.axis_size(axis), x.shape[dim])
        up = [(i, (i + 1) % devices) for i in range(devices)]
        down = [(j, i) for i, j in up]
        last = lax.slice_in_dim(x, length - width, length, axis=dim)
        initial = lax.slice_in_dim(x, 0, width, axis=dim)
        before = lax.ppermute(last, axis, up)
        after = lax.ppermute(initial, axis, down)
        x = jnp.concatenate([before, x, after], axis=dim)
    return x


def from_partner(value, axis, stride):
    mask = 2**stride
    pairs = [(source, source ^ mask) for source in range(lax.axis_size(axis))]
    return lax.ppermute(value, axis, pairs)


def velocity_values(indices, extent):
    return (indices.astype(jnp.float32) - (extent - 1) / 2.0) * VELOCITY_STEP


def plane_speed(indices, extent):
    return CFL_NUMBER * (2 * indices - (extent - 1)).astype(jnp.float32) / (extent - 1)


def velocity_index(positions, extent):
    half = extent // 2
    return jnp.where(positions < half, positions, 3 * half - 1 - positions)


def tables(row_index, col_index, extent):
    phases = row_index[:, None] * col_index[None, :] % extent
    angles = phases.astype(jnp.float32) * (2.0 * math.pi / extent)
    return (jnp.cos(angles), jnp.sin(angles))


def multiply(table, operand):
    return jnp.einsum("ka,bam->bkm", table, operand, precision=lax.Precision.HIGHEST)


def rotate(operand, extent_mid, extent_low):
    batch_count, extent_top, merged = operand.shape
    shaped = operand.reshape(batch_count, extent_top, extent_mid, extent_low)
    return jnp.transpose(shaped, (0, 2, 3, 1)).reshape(
        batch_count, extent_mid, extent_low * extent_top
    )


def spectral(real_in, imag_in, orient, real_only):
    extents = (NVX, NVY, NVZ)
    real_now = real_in
    imag_now = imag_in
    for pass_index in range(3):
        extent = extents[pass_index]
        extent_mid = extents[(pass_index + 1) % 3]
        extent_low = extents[(pass_index + 2) % 3]
        plain = jnp.arange(extent, dtype=jnp.int32)
        if pass_index == 0 and orient < 0:
            cosines, sines = tables(plain, velocity_index(plain, extent), extent)
        elif pass_index == 0:
            cosines, sines = tables(velocity_index(plain, extent), plain, extent)
        else:
            cosines, sines = tables(plain, plain, extent)
        final_pass = real_only and pass_index == 2
        if imag_now is None:
            real_next = multiply(cosines, real_now)
            imag_next = orient * multiply(sines, real_now)
        else:
            real_next = multiply(cosines, real_now) - orient * multiply(sines, imag_now)
            if final_pass:
                imag_next = None
            else:
                imag_next = multiply(cosines, imag_now) + orient * multiply(sines, real_now)
        real_now = rotate(real_next, extent_mid, extent_low)
        imag_now = None if imag_next is None else rotate(imag_next, extent_mid, extent_low)
    return (real_now, imag_now)


def collide(heavy_block, fourier_scattering_table):
    species_count, x_extent_size, cell_count, merged = heavy_block.shape
    flattened = jnp.transpose(heavy_block, (0, 2, 1, 3)).reshape(
        species_count * cell_count, x_extent_size, merged
    )
    spec_real, spec_imag = spectral(flattened, None, -1, False)

    def invert(kernel_index):
        kernel = fourier_scattering_table[kernel_index][None, :, :]
        real_out, unused = spectral(spec_real * kernel, spec_imag * kernel, 1, True)
        return real_out / (NVX * NVY * NVZ)

    gain_sum = invert(0) * invert(1)
    loss_term = flattened * invert(2 * PAIRS)
    updated = flattened + COLLIDE_SCALE * (gain_sum - loss_term)
    return jnp.transpose(
        updated.reshape(species_count, cell_count, x_extent_size, merged), (0, 2, 1, 3)
    )


def advance(padded, mirror, odd_stiffness_factor, leading_plane, x_extent_size):
    planes = padded.shape[1]
    positions = leading_plane + jnp.arange(planes, dtype=jnp.int32)
    speeds = plane_speed(velocity_index(positions, x_extent_size), x_extent_size)[
        None, :, None, None
    ]
    even_part = 0.5 * (padded + mirror)
    odd_part = 0.5 * (padded - mirror)
    even_diff = 0.5 * (even_part[:, :, 2:] - even_part[:, :, :-2])
    odd_diff = 0.5 * (odd_part[:, :, 2:] - odd_part[:, :, :-2])
    even_new = even_part[:, :, 1:-1] - speeds * odd_diff
    odd_new = (odd_part[:, :, 1:-1] - speeds * even_diff) / (1.0 + odd_stiffness_factor)[
        :, None, None, None
    ]
    return even_new + odd_new


def moments(light_portion, leading_plane, x_extent_size):
    planes = light_portion.shape[1]
    positions = leading_plane + jnp.arange(planes, dtype=jnp.int32)
    along_first = velocity_values(velocity_index(positions, x_extent_size), x_extent_size)
    along_second = jnp.repeat(velocity_values(jnp.arange(NVY, dtype=jnp.int32), NVY), NVZ)
    along_third = jnp.tile(velocity_values(jnp.arange(NVZ, dtype=jnp.int32), NVZ), NVY)
    density = jnp.sum(light_portion, axis=(1, 3))
    moment_first = jnp.sum(light_portion * along_first[None, :, None, None], axis=(1, 3))
    moment_second = jnp.sum(light_portion * along_second, axis=(1, 3))
    moment_third = jnp.sum(light_portion * along_third, axis=(1, 3))
    return jnp.stack([density, moment_first, moment_second, moment_third])


def relax_light_species(
    light_portion,
    summed_moments,
    leading_plane,
    x_extent_size,
    electron_bgk_frequency_dt,
    electron_kinetic_heat_level,
):
    light_count, planes, cell_count, merged = light_portion.shape
    density = summed_moments[0]
    drifts = summed_moments[1:] / density[None]
    equilibrium_heat_level = electron_kinetic_heat_level[:, None, None]

    def integration_coefficient(values, drift):
        offset_counts_per_row = values[None, None, :] - drift[:, :, None]
        return jnp.exp(
            -(offset_counts_per_row * offset_counts_per_row) / (2.0 * equilibrium_heat_level)
        )

    def profile(values, drift):
        weights = integration_coefficient(values, drift)
        return weights / jnp.sum(weights, axis=2, keepdims=True)

    full_first = integration_coefficient(
        velocity_values(jnp.arange(x_extent_size, dtype=jnp.int32), x_extent_size), drifts[0]
    )
    positions = leading_plane + jnp.arange(planes, dtype=jnp.int32)
    local_values = velocity_values(velocity_index(positions, x_extent_size), x_extent_size)
    local_first = integration_coefficient(local_values, drifts[0]) / jnp.sum(
        full_first, axis=2, keepdims=True
    )
    grid_second = velocity_values(jnp.arange(NVY, dtype=jnp.int32), NVY)
    grid_third = velocity_values(jnp.arange(NVZ, dtype=jnp.int32), NVZ)
    profile_rest = (
        profile(grid_second, drifts[1])[:, :, :, None]
        * profile(grid_third, drifts[2])[:, :, None, :]
    ).reshape(light_count, cell_count, merged)
    maxwell = (
        density[:, None, :, None]
        * jnp.transpose(local_first, (0, 2, 1))[:, :, :, None]
        * profile_rest[:, None, :, :]
    )
    rates = electron_bgk_frequency_dt[:, None, None, None]
    return (light_portion + rates * maxwell) / (1.0 + rates)


def body(
    phase_density_field,
    fourier_scattering_table,
    odd_stiffness_factor,
    electron_bgk_frequency_dt,
    electron_kinetic_heat_level,
):
    species_count = phase_density_field.shape[0]
    heavy_count = species_count - electron_bgk_frequency_dt.shape[0]
    x_extent_size = fourier_scattering_table.shape[1]
    planes = phase_density_field.shape[1]
    padded = extended(phase_density_field, (("space", 2),), 1)
    leading_plane = lax.axis_index("vel") * planes
    positions = leading_plane + jnp.arange(planes, dtype=jnp.int32)
    speeds = plane_speed(velocity_index(positions, x_extent_size), x_extent_size)[
        None, :, None, None
    ]
    shifted = phase_density_field - speeds * (
        0.5 * (padded[:, :, 2:] - padded[:, :, :-2])
    )
    gathered = lax.all_to_all(shifted, "vel", split_axis=2, concat_axis=1, tiled=True)
    half = x_extent_size // 2
    mirror = jnp.flip(
        jnp.concatenate([gathered[:, half:], gathered[:, :half]], axis=1), axis=3
    )
    ratio = 1.0 / (1.0 + odd_stiffness_factor)
    alpha = (0.5 * (1.0 + ratio))[:, None, None, None]
    beta = (0.5 * (1.0 - ratio))[:, None, None, None]
    advanced = alpha * gathered + beta * mirror
    heavy_part = collide(advanced[:heavy_count], fourier_scattering_table)
    light_portion = advanced[heavy_count:]
    summed_moments = moments(light_portion, 0, x_extent_size)
    light_portion = relax_light_species(
        light_portion,
        summed_moments,
        0,
        x_extent_size,
        electron_bgk_frequency_dt,
        electron_kinetic_heat_level,
    )
    result = jnp.concatenate([heavy_part, light_portion], axis=0)
    return lax.all_to_all(result, "vel", split_axis=1, concat_axis=2, tiled=True)


def solution(mesh):
    in_specs = (P(None, "vel", "space", None), P(), P(), P(), P())
    out_specs = P(None, "vel", "space", None)
    return jax.shard_map(body, mesh=mesh, in_specs=in_specs, out_specs=out_specs, check_vma=False)
```

```python
import math

import jax
import jax.numpy as jnp
from jax import lax
from jax.sharding import PartitionSpec as P

NVX = 32
NVY = 32
NVZ = 32
PAIRS = 1


CFL_NUMBER = 0.2
VELOCITY_STEP = 0.375
COLLIDE_SCALE = 0.25


def extended(x, sides, width):
    for axis, dim in sides:
        devices, length = (lax.axis_size(axis), x.shape[dim])
        up = [(i, (i + 1) % devices) for i in range(devices)]
        down = [(j, i) for i, j in up]
        last = lax.slice_in_dim(x, length - width, length, axis=dim)
        initial = lax.slice_in_dim(x, 0, width, axis=dim)
        before = lax.ppermute(last, axis, up)
        after = lax.ppermute(initial, axis, down)
        x = jnp.concatenate([before, x, after], axis=dim)
    return x


def from_partner(value, axis, stride):
    mask = 2**stride
    pairs = [(source, source ^ mask) for source in range(lax.axis_size(axis))]
    return lax.ppermute(value, axis, pairs)


def velocity_values(indices, extent):
    return (indices.astype(jnp.float32) - (extent - 1) / 2.0) * VELOCITY_STEP


def plane_speed(indices, extent):
    return CFL_NUMBER * (2 * indices - (extent - 1)).astype(jnp.float32) / (extent - 1)


def velocity_index(positions, extent):
    half = extent // 2
    return jnp.where(positions < half, positions, 3 * half - 1 - positions)


def tables(row_index, col_index, extent):
    phases = row_index[:, None] * col_index[None, :] % extent
    angles = phases.astype(jnp.float32) * (2.0 * math.pi / extent)
    return (jnp.cos(angles), jnp.sin(angles))


def multiply(table, operand):
    return jnp.einsum("ka,bam->bkm", table, operand, precision=lax.Precision.HIGHEST)


def rotate(operand, extent_mid, extent_low):
    batch_count, extent_top, merged = operand.shape
    shaped = operand.reshape(batch_count, extent_top, extent_mid, extent_low)
    return jnp.transpose(shaped, (0, 2, 3, 1)).reshape(
        batch_count, extent_mid, extent_low * extent_top
    )


def spectral(real_in, imag_in, orient, real_only):
    extents = (NVX, NVY, NVZ)
    real_now = real_in
    imag_now = imag_in
    for pass_index in range(3):
        extent = extents[pass_index]
        extent_mid = extents[(pass_index + 1) % 3]
        extent_low = extents[(pass_index + 2) % 3]
        plain = jnp.arange(extent, dtype=jnp.int32)
        if pass_index == 0 and orient < 0:
            cosines, sines = tables(plain, velocity_index(plain, extent), extent)
        elif pass_index == 0:
            cosines, sines = tables(velocity_index(plain, extent), plain, extent)
        else:
            cosines, sines = tables(plain, plain, extent)
        final_pass = real_only and pass_index == 2
        if imag_now is None:
            real_next = multiply(cosines, real_now)
            imag_next = orient * multiply(sines, real_now)
        else:
            real_next = multiply(cosines, real_now) - orient * multiply(sines, imag_now)
            if final_pass:
                imag_next = None
            else:
                imag_next = multiply(cosines, imag_now) + orient * multiply(sines, real_now)
        real_now = rotate(real_next, extent_mid, extent_low)
        imag_now = None if imag_next is None else rotate(imag_next, extent_mid, extent_low)
    return (real_now, imag_now)


def collide(heavy_block, fourier_scattering_table):
    species_count, x_extent_size, cell_count, merged = heavy_block.shape
    flattened = jnp.transpose(heavy_block, (0, 2, 1, 3)).reshape(
        species_count * cell_count, x_extent_size, merged
    )
    spec_real, spec_imag = spectral(flattened, None, -1, False)

    def invert(kernel_index):
        kernel = fourier_scattering_table[kernel_index][None, :, :]
        real_out, unused = spectral(spec_real * kernel, spec_imag * kernel, 1, True)
        return real_out / (NVX * NVY * NVZ)

    gain_sum = invert(0) * invert(1)
    loss_term = flattened * invert(2 * PAIRS)
    updated = flattened + COLLIDE_SCALE * (gain_sum - loss_term)
    return jnp.transpose(
        updated.reshape(species_count, cell_count, x_extent_size, merged), (0, 2, 1, 3)
    )


def split_bf16(values):
    rounded = lax.reduce_precision(values, exponent_bits=8, mantissa_bits=7)
    return rounded.astype(jnp.bfloat16), (values - rounded).astype(jnp.bfloat16)


def kron_tables(extent):
    size = extent * extent
    rows, cols = lax.optimization_barrier(
        (
            lax.broadcasted_iota(jnp.int32, (size, 1), 0),
            lax.broadcasted_iota(jnp.int32, (1, size), 1),
        )
    )
    phases = ((rows // extent) * (cols // extent) + (rows % extent) * (cols % extent)) % extent
    angles = phases.astype(jnp.float32) * (2.0 * math.pi / extent)
    return split_bf16(jnp.cos(angles)), split_bf16(jnp.sin(angles))


def split_dot(operand, table):
    high, low = table
    op_high, op_low = split_bf16(operand)

    def dot(left, right):
        return jnp.dot(left, right, preferred_element_type=jnp.float32)

    return dot(op_high, high) + (dot(op_low, high) + dot(op_high, low))


def collide_kron(heavy_block, fourier_scattering_table):
    species_count, x_extent_size, cell_count, merged = heavy_block.shape
    hp = lax.Precision.HIGHEST
    flat = jnp.transpose(heavy_block, (0, 2, 1, 3)).reshape(
        species_count * cell_count, x_extent_size, merged
    )
    plain = jnp.arange(x_extent_size, dtype=jnp.int32)
    x_cos, x_sin = tables(plain, velocity_index(plain, x_extent_size), x_extent_size)
    wide_cos, wide_sin = kron_tables(NVY)
    rows = species_count * cell_count
    x_real = jnp.einsum("kp,bpm->kbm", x_cos, flat, precision=hp)
    x_imag = -jnp.einsum("kp,bpm->kbm", x_sin, flat, precision=hp)
    stacked = jnp.concatenate([x_real, x_imag], axis=1).reshape(-1, merged)
    by_cos = split_dot(stacked, wide_cos).reshape(x_extent_size, 2, rows, merged)
    by_sin = split_dot(stacked, wide_sin).reshape(x_extent_size, 2, rows, merged)
    spec_real = by_cos[:, 0] + by_sin[:, 1]
    spec_imag = by_cos[:, 1] - by_sin[:, 0]
    kernels = jnp.transpose(fourier_scattering_table, (1, 0, 2))[:, :, None, :]
    z_real = kernels * spec_real[:, None]
    z_imag = kernels * spec_imag[:, None]
    u_real = jnp.einsum("kp,kqbm->pqbm", x_cos, z_real, precision=hp) - jnp.einsum(
        "kp,kqbm->pqbm", x_sin, z_imag, precision=hp
    )
    u_imag = jnp.einsum("kp,kqbm->pqbm", x_sin, z_real, precision=hp) + jnp.einsum(
        "kp,kqbm->pqbm", x_cos, z_imag, precision=hp
    )
    parts = (
        split_dot(u_real.reshape(-1, merged), wide_cos)
        - split_dot(u_imag.reshape(-1, merged), wide_sin)
    ).reshape(
        x_extent_size, fourier_scattering_table.shape[0], rows, merged
    ) / (NVX * NVY * NVZ)
    fields = jnp.transpose(flat, (1, 0, 2))
    updated = fields + COLLIDE_SCALE * (parts[:, 0] * parts[:, 1] - fields * parts[:, 2])
    return jnp.transpose(
        updated.reshape(x_extent_size, species_count, cell_count, merged), (1, 0, 2, 3)
    )


def advance(padded, mirror, odd_stiffness_factor, leading_plane, x_extent_size):
    planes = padded.shape[1]
    positions = leading_plane + jnp.arange(planes, dtype=jnp.int32)
    speeds = plane_speed(velocity_index(positions, x_extent_size), x_extent_size)[
        None, :, None, None
    ]
    even_part = 0.5 * (padded + mirror)
    odd_part = 0.5 * (padded - mirror)
    even_diff = 0.5 * (even_part[:, :, 2:] - even_part[:, :, :-2])
    odd_diff = 0.5 * (odd_part[:, :, 2:] - odd_part[:, :, :-2])
    even_new = even_part[:, :, 1:-1] - speeds * odd_diff
    odd_new = (odd_part[:, :, 1:-1] - speeds * even_diff) / (1.0 + odd_stiffness_factor)[
        :, None, None, None
    ]
    return even_new + odd_new


def moments(light_portion, leading_plane, x_extent_size):
    planes = light_portion.shape[1]
    positions = leading_plane + jnp.arange(planes, dtype=jnp.int32)
    along_first = velocity_values(velocity_index(positions, x_extent_size), x_extent_size)
    along_second = jnp.repeat(velocity_values(jnp.arange(NVY, dtype=jnp.int32), NVY), NVZ)
    along_third = jnp.tile(velocity_values(jnp.arange(NVZ, dtype=jnp.int32), NVZ), NVY)
    density = jnp.sum(light_portion, axis=(1, 3))
    moment_first = jnp.sum(light_portion * along_first[None, :, None, None], axis=(1, 3))
    moment_second = jnp.sum(light_portion * along_second, axis=(1, 3))
    moment_third = jnp.sum(light_portion * along_third, axis=(1, 3))
    return jnp.stack([density, moment_first, moment_second, moment_third])


def relax_light_species(
    light_portion,
    summed_moments,
    leading_plane,
    x_extent_size,
    electron_bgk_frequency_dt,
    electron_kinetic_heat_level,
):
    light_count, planes, cell_count, merged = light_portion.shape
    density = summed_moments[0]
    drifts = summed_moments[1:] / density[None]
    equilibrium_heat_level = electron_kinetic_heat_level[:, None, None]

    def integration_coefficient(values, drift):
        offset_counts_per_row = values[None, None, :] - drift[:, :, None]
        return jnp.exp(
            -(offset_counts_per_row * offset_counts_per_row) / (2.0 * equilibrium_heat_level)
        )

    def profile(values, drift):
        weights = integration_coefficient(values, drift)
        return weights / jnp.sum(weights, axis=2, keepdims=True)

    full_first = integration_coefficient(
        velocity_values(jnp.arange(x_extent_size, dtype=jnp.int32), x_extent_size), drifts[0]
    )
    positions = leading_plane + jnp.arange(planes, dtype=jnp.int32)
    local_values = velocity_values(velocity_index(positions, x_extent_size), x_extent_size)
    local_first = integration_coefficient(local_values, drifts[0]) / jnp.sum(
        full_first, axis=2, keepdims=True
    )
    grid_second = velocity_values(jnp.arange(NVY, dtype=jnp.int32), NVY)
    grid_third = velocity_values(jnp.arange(NVZ, dtype=jnp.int32), NVZ)
    profile_rest = (
        profile(grid_second, drifts[1])[:, :, :, None]
        * profile(grid_third, drifts[2])[:, :, None, :]
    ).reshape(light_count, cell_count, merged)
    maxwell = (
        density[:, None, :, None]
        * jnp.transpose(local_first, (0, 2, 1))[:, :, :, None]
        * profile_rest[:, None, :, :]
    )
    rates = electron_bgk_frequency_dt[:, None, None, None]
    return (light_portion + rates * maxwell) / (1.0 + rates)


def body(
    phase_density_field,
    fourier_scattering_table,
    odd_stiffness_factor,
    electron_bgk_frequency_dt,
    electron_kinetic_heat_level,
):
    species_count = phase_density_field.shape[0]
    heavy_count = species_count - electron_bgk_frequency_dt.shape[0]
    x_extent_size = fourier_scattering_table.shape[1]
    planes = phase_density_field.shape[1]
    padded = extended(phase_density_field, (("space", 2),), 1)
    leading_plane = lax.axis_index("vel") * planes
    positions = leading_plane + jnp.arange(planes, dtype=jnp.int32)
    speeds = plane_speed(velocity_index(positions, x_extent_size), x_extent_size)[
        None, :, None, None
    ]
    shifted = phase_density_field - speeds * (
        0.5 * (padded[:, :, 2:] - padded[:, :, :-2])
    )
    gathered = lax.all_to_all(shifted, "vel", split_axis=2, concat_axis=1, tiled=True)
    half = x_extent_size // 2
    mirror = jnp.flip(
        jnp.concatenate([gathered[:, half:], gathered[:, :half]], axis=1), axis=3
    )
    ratio = 1.0 / (1.0 + odd_stiffness_factor)
    alpha = (0.5 * (1.0 + ratio))[:, None, None, None]
    beta = (0.5 * (1.0 - ratio))[:, None, None, None]
    advanced = alpha * gathered + beta * mirror
    heavy_part = collide_kron(advanced[:heavy_count], fourier_scattering_table)
    light_portion = advanced[heavy_count:]
    summed_moments = moments(light_portion, 0, x_extent_size)
    light_portion = relax_light_species(
        light_portion,
        summed_moments,
        0,
        x_extent_size,
        electron_bgk_frequency_dt,
        electron_kinetic_heat_level,
    )
    result = jnp.concatenate([heavy_part, light_portion], axis=0)
    return lax.all_to_all(result, "vel", split_axis=1, concat_axis=2, tiled=True)


def solution(mesh):
    in_specs = (P(None, "vel", "space", None), P(), P(), P(), P())
    out_specs = P(None, "vel", "space", None)
    return jax.shard_map(body, mesh=mesh, in_specs=in_specs, out_specs=out_specs, check_vma=False)
```

```python
import math

import numpy as np

import jax
import jax.numpy as jnp
from jax import lax
from jax.sharding import PartitionSpec as P

NVX = 32
NVY = 32
NVZ = 32
PAIRS = 1


CFL_NUMBER = 0.2
VELOCITY_STEP = 0.375
COLLIDE_SCALE = 0.25


def extended(x, sides, width):
    for axis, dim in sides:
        devices, length = (lax.axis_size(axis), x.shape[dim])
        up = [(i, (i + 1) % devices) for i in range(devices)]
        down = [(j, i) for i, j in up]
        last = lax.slice_in_dim(x, length - width, length, axis=dim)
        initial = lax.slice_in_dim(x, 0, width, axis=dim)
        before = lax.ppermute(last, axis, up)
        after = lax.ppermute(initial, axis, down)
        x = jnp.concatenate([before, x, after], axis=dim)
    return x


def from_partner(value, axis, stride):
    mask = 2**stride
    pairs = [(source, source ^ mask) for source in range(lax.axis_size(axis))]
    return lax.ppermute(value, axis, pairs)


def velocity_values(indices, extent):
    return (indices.astype(jnp.float32) - (extent - 1) / 2.0) * VELOCITY_STEP


def plane_speed(indices, extent):
    return CFL_NUMBER * (2 * indices - (extent - 1)).astype(jnp.float32) / (extent - 1)


def velocity_index(positions, extent):
    half = extent // 2
    return jnp.where(positions < half, positions, 3 * half - 1 - positions)


def tables(row_index, col_index, extent):
    phases = row_index[:, None] * col_index[None, :] % extent
    angles = phases.astype(jnp.float32) * (2.0 * math.pi / extent)
    return (jnp.cos(angles), jnp.sin(angles))


def multiply(table, operand):
    return jnp.einsum("ka,bam->bkm", table, operand, precision=lax.Precision.HIGHEST)


def rotate(operand, extent_mid, extent_low):
    batch_count, extent_top, merged = operand.shape
    shaped = operand.reshape(batch_count, extent_top, extent_mid, extent_low)
    return jnp.transpose(shaped, (0, 2, 3, 1)).reshape(
        batch_count, extent_mid, extent_low * extent_top
    )


def spectral(real_in, imag_in, orient, real_only):
    extents = (NVX, NVY, NVZ)
    real_now = real_in
    imag_now = imag_in
    for pass_index in range(3):
        extent = extents[pass_index]
        extent_mid = extents[(pass_index + 1) % 3]
        extent_low = extents[(pass_index + 2) % 3]
        plain = jnp.arange(extent, dtype=jnp.int32)
        if pass_index == 0 and orient < 0:
            cosines, sines = tables(plain, velocity_index(plain, extent), extent)
        elif pass_index == 0:
            cosines, sines = tables(velocity_index(plain, extent), plain, extent)
        else:
            cosines, sines = tables(plain, plain, extent)
        final_pass = real_only and pass_index == 2
        if imag_now is None:
            real_next = multiply(cosines, real_now)
            imag_next = orient * multiply(sines, real_now)
        else:
            real_next = multiply(cosines, real_now) - orient * multiply(sines, imag_now)
            if final_pass:
                imag_next = None
            else:
                imag_next = multiply(cosines, imag_now) + orient * multiply(sines, real_now)
        real_now = rotate(real_next, extent_mid, extent_low)
        imag_now = None if imag_next is None else rotate(imag_next, extent_mid, extent_low)
    return (real_now, imag_now)


def collide(heavy_block, fourier_scattering_table):
    species_count, x_extent_size, cell_count, merged = heavy_block.shape
    flattened = jnp.transpose(heavy_block, (0, 2, 1, 3)).reshape(
        species_count * cell_count, x_extent_size, merged
    )
    spec_real, spec_imag = spectral(flattened, None, -1, False)

    def invert(kernel_index):
        kernel = fourier_scattering_table[kernel_index][None, :, :]
        real_out, unused = spectral(spec_real * kernel, spec_imag * kernel, 1, True)
        return real_out / (NVX * NVY * NVZ)

    gain_sum = invert(0) * invert(1)
    loss_term = flattened * invert(2 * PAIRS)
    updated = flattened + COLLIDE_SCALE * (gain_sum - loss_term)
    return jnp.transpose(
        updated.reshape(species_count, cell_count, x_extent_size, merged), (0, 2, 1, 3)
    )


def split_bf16(values):
    rounded = lax.reduce_precision(values, exponent_bits=8, mantissa_bits=7)
    return rounded.astype(jnp.bfloat16), (values - rounded).astype(jnp.bfloat16)


def kron_tables(extent):
    size = extent * extent
    index = np.arange(size)
    phases = (
        np.outer(index // extent, index // extent) + np.outer(index % extent, index % extent)
    ) % extent
    angles = phases * (2.0 * np.pi / extent)

    def split(values):
        high = values.astype(jnp.bfloat16)
        low = (values - high.astype(np.float64)).astype(jnp.bfloat16)
        return jnp.asarray(high), jnp.asarray(low)

    return split(np.cos(angles)), split(np.sin(angles))


def split_dot(operand, table):
    high, low = table
    op_high, op_low = split_bf16(operand)

    def dot(left, right):
        return jnp.dot(left, right, preferred_element_type=jnp.float32)

    return dot(op_high, high) + (dot(op_low, high) + dot(op_high, low))


def collide_kron(heavy_block, fourier_scattering_table):
    species_count, x_extent_size, cell_count, merged = heavy_block.shape
    hp = lax.Precision.HIGHEST
    flat = jnp.transpose(heavy_block, (0, 2, 1, 3)).reshape(
        species_count * cell_count, x_extent_size, merged
    )
    plain = jnp.arange(x_extent_size, dtype=jnp.int32)
    x_cos, x_sin = tables(plain, velocity_index(plain, x_extent_size), x_extent_size)
    wide_cos, wide_sin = kron_tables(NVY)
    rows = species_count * cell_count
    x_real = jnp.einsum("kp,bpm->kbm", x_cos, flat, precision=hp)
    x_imag = -jnp.einsum("kp,bpm->kbm", x_sin, flat, precision=hp)
    stacked = jnp.concatenate([x_real, x_imag], axis=1).reshape(-1, merged)
    by_cos = split_dot(stacked, wide_cos).reshape(x_extent_size, 2, rows, merged)
    by_sin = split_dot(stacked, wide_sin).reshape(x_extent_size, 2, rows, merged)
    spec_real = by_cos[:, 0] + by_sin[:, 1]
    spec_imag = by_cos[:, 1] - by_sin[:, 0]
    kernels = jnp.transpose(fourier_scattering_table, (1, 0, 2))[:, :, None, :]
    z_real = kernels * spec_real[:, None]
    z_imag = kernels * spec_imag[:, None]
    u_real = jnp.einsum("kp,kqbm->pqbm", x_cos, z_real, precision=hp) - jnp.einsum(
        "kp,kqbm->pqbm", x_sin, z_imag, precision=hp
    )
    u_imag = jnp.einsum("kp,kqbm->pqbm", x_sin, z_real, precision=hp) + jnp.einsum(
        "kp,kqbm->pqbm", x_cos, z_imag, precision=hp
    )
    parts = (
        split_dot(u_real.reshape(-1, merged), wide_cos)
        - split_dot(u_imag.reshape(-1, merged), wide_sin)
    ).reshape(
        x_extent_size, fourier_scattering_table.shape[0], rows, merged
    ) / (NVX * NVY * NVZ)
    fields = jnp.transpose(flat, (1, 0, 2))
    updated = fields + COLLIDE_SCALE * (parts[:, 0] * parts[:, 1] - fields * parts[:, 2])
    return jnp.transpose(
        updated.reshape(x_extent_size, species_count, cell_count, merged), (1, 0, 2, 3)
    )


def advance(padded, mirror, odd_stiffness_factor, leading_plane, x_extent_size):
    planes = padded.shape[1]
    positions = leading_plane + jnp.arange(planes, dtype=jnp.int32)
    speeds = plane_speed(velocity_index(positions, x_extent_size), x_extent_size)[
        None, :, None, None
    ]
    even_part = 0.5 * (padded + mirror)
    odd_part = 0.5 * (padded - mirror)
    even_diff = 0.5 * (even_part[:, :, 2:] - even_part[:, :, :-2])
    odd_diff = 0.5 * (odd_part[:, :, 2:] - odd_part[:, :, :-2])
    even_new = even_part[:, :, 1:-1] - speeds * odd_diff
    odd_new = (odd_part[:, :, 1:-1] - speeds * even_diff) / (1.0 + odd_stiffness_factor)[
        :, None, None, None
    ]
    return even_new + odd_new


def moments(light_portion, leading_plane, x_extent_size):
    planes = light_portion.shape[1]
    positions = leading_plane + jnp.arange(planes, dtype=jnp.int32)
    along_first = velocity_values(velocity_index(positions, x_extent_size), x_extent_size)
    along_second = jnp.repeat(velocity_values(jnp.arange(NVY, dtype=jnp.int32), NVY), NVZ)
    along_third = jnp.tile(velocity_values(jnp.arange(NVZ, dtype=jnp.int32), NVZ), NVY)
    density = jnp.sum(light_portion, axis=(1, 3))
    moment_first = jnp.sum(light_portion * along_first[None, :, None, None], axis=(1, 3))
    moment_second = jnp.sum(light_portion * along_second, axis=(1, 3))
    moment_third = jnp.sum(light_portion * along_third, axis=(1, 3))
    return jnp.stack([density, moment_first, moment_second, moment_third])


def relax_light_species(
    light_portion,
    summed_moments,
    leading_plane,
    x_extent_size,
    electron_bgk_frequency_dt,
    electron_kinetic_heat_level,
):
    light_count, planes, cell_count, merged = light_portion.shape
    density = summed_moments[0]
    drifts = summed_moments[1:] / density[None]
    equilibrium_heat_level = electron_kinetic_heat_level[:, None, None]

    def integration_coefficient(values, drift):
        offset_counts_per_row = values[None, None, :] - drift[:, :, None]
        return jnp.exp(
            -(offset_counts_per_row * offset_counts_per_row) / (2.0 * equilibrium_heat_level)
        )

    def profile(values, drift):
        weights = integration_coefficient(values, drift)
        return weights / jnp.sum(weights, axis=2, keepdims=True)

    full_first = integration_coefficient(
        velocity_values(jnp.arange(x_extent_size, dtype=jnp.int32), x_extent_size), drifts[0]
    )
    positions = leading_plane + jnp.arange(planes, dtype=jnp.int32)
    local_values = velocity_values(velocity_index(positions, x_extent_size), x_extent_size)
    local_first = integration_coefficient(local_values, drifts[0]) / jnp.sum(
        full_first, axis=2, keepdims=True
    )
    grid_second = velocity_values(jnp.arange(NVY, dtype=jnp.int32), NVY)
    grid_third = velocity_values(jnp.arange(NVZ, dtype=jnp.int32), NVZ)
    profile_rest = (
        profile(grid_second, drifts[1])[:, :, :, None]
        * profile(grid_third, drifts[2])[:, :, None, :]
    ).reshape(light_count, cell_count, merged)
    maxwell = (
        density[:, None, :, None]
        * jnp.transpose(local_first, (0, 2, 1))[:, :, :, None]
        * profile_rest[:, None, :, :]
    )
    rates = electron_bgk_frequency_dt[:, None, None, None]
    return (light_portion + rates * maxwell) / (1.0 + rates)


def body(
    phase_density_field,
    fourier_scattering_table,
    odd_stiffness_factor,
    electron_bgk_frequency_dt,
    electron_kinetic_heat_level,
):
    species_count = phase_density_field.shape[0]
    heavy_count = species_count - electron_bgk_frequency_dt.shape[0]
    x_extent_size = fourier_scattering_table.shape[1]
    planes = phase_density_field.shape[1]
    padded = extended(phase_density_field, (("space", 2),), 1)
    leading_plane = lax.axis_index("vel") * planes
    positions = leading_plane + jnp.arange(planes, dtype=jnp.int32)
    speeds = plane_speed(velocity_index(positions, x_extent_size), x_extent_size)[
        None, :, None, None
    ]
    shifted = phase_density_field - speeds * (
        0.5 * (padded[:, :, 2:] - padded[:, :, :-2])
    )
    gathered = lax.all_to_all(shifted, "vel", split_axis=2, concat_axis=1, tiled=True)
    half = x_extent_size // 2
    mirror = jnp.flip(
        jnp.concatenate([gathered[:, half:], gathered[:, :half]], axis=1), axis=3
    )
    ratio = 1.0 / (1.0 + odd_stiffness_factor)
    alpha = (0.5 * (1.0 + ratio))[:, None, None, None]
    beta = (0.5 * (1.0 - ratio))[:, None, None, None]
    advanced = alpha * gathered + beta * mirror
    heavy_part = collide_kron(advanced[:heavy_count], fourier_scattering_table)
    light_portion = advanced[heavy_count:]
    summed_moments = moments(light_portion, 0, x_extent_size)
    light_portion = relax_light_species(
        light_portion,
        summed_moments,
        0,
        x_extent_size,
        electron_bgk_frequency_dt,
        electron_kinetic_heat_level,
    )
    result = jnp.concatenate([heavy_part, light_portion], axis=0)
    return lax.all_to_all(result, "vel", split_axis=1, concat_axis=2, tiled=True)


def solution(mesh):
    in_specs = (P(None, "vel", "space", None), P(), P(), P(), P())
    out_specs = P(None, "vel", "space", None)
    return jax.shard_map(body, mesh=mesh, in_specs=in_specs, out_specs=out_specs, check_vma=False)
```

```python
import math

import numpy as np

import jax
import jax.numpy as jnp
from jax import lax
from jax.sharding import PartitionSpec as P

NVX = 32
NVY = 32
NVZ = 32
PAIRS = 1


CFL_NUMBER = 0.2
VELOCITY_STEP = 0.375
COLLIDE_SCALE = 0.25


def extended(x, sides, width):
    for axis, dim in sides:
        devices, length = (lax.axis_size(axis), x.shape[dim])
        up = [(i, (i + 1) % devices) for i in range(devices)]
        down = [(j, i) for i, j in up]
        last = lax.slice_in_dim(x, length - width, length, axis=dim)
        initial = lax.slice_in_dim(x, 0, width, axis=dim)
        before = lax.ppermute(last, axis, up)
        after = lax.ppermute(initial, axis, down)
        x = jnp.concatenate([before, x, after], axis=dim)
    return x


def from_partner(value, axis, stride):
    mask = 2**stride
    pairs = [(source, source ^ mask) for source in range(lax.axis_size(axis))]
    return lax.ppermute(value, axis, pairs)


def velocity_values(indices, extent):
    return (indices.astype(jnp.float32) - (extent - 1) / 2.0) * VELOCITY_STEP


def plane_speed(indices, extent):
    return CFL_NUMBER * (2 * indices - (extent - 1)).astype(jnp.float32) / (extent - 1)


def velocity_index(positions, extent):
    half = extent // 2
    return jnp.where(positions < half, positions, 3 * half - 1 - positions)


def tables(row_index, col_index, extent):
    phases = row_index[:, None] * col_index[None, :] % extent
    angles = phases.astype(jnp.float32) * (2.0 * math.pi / extent)
    return (jnp.cos(angles), jnp.sin(angles))


def multiply(table, operand):
    return jnp.einsum("ka,bam->bkm", table, operand, precision=lax.Precision.HIGHEST)


def rotate(operand, extent_mid, extent_low):
    batch_count, extent_top, merged = operand.shape
    shaped = operand.reshape(batch_count, extent_top, extent_mid, extent_low)
    return jnp.transpose(shaped, (0, 2, 3, 1)).reshape(
        batch_count, extent_mid, extent_low * extent_top
    )


def spectral(real_in, imag_in, orient, real_only):
    extents = (NVX, NVY, NVZ)
    real_now = real_in
    imag_now = imag_in
    for pass_index in range(3):
        extent = extents[pass_index]
        extent_mid = extents[(pass_index + 1) % 3]
        extent_low = extents[(pass_index + 2) % 3]
        plain = jnp.arange(extent, dtype=jnp.int32)
        if pass_index == 0 and orient < 0:
            cosines, sines = tables(plain, velocity_index(plain, extent), extent)
        elif pass_index == 0:
            cosines, sines = tables(velocity_index(plain, extent), plain, extent)
        else:
            cosines, sines = tables(plain, plain, extent)
        final_pass = real_only and pass_index == 2
        if imag_now is None:
            real_next = multiply(cosines, real_now)
            imag_next = orient * multiply(sines, real_now)
        else:
            real_next = multiply(cosines, real_now) - orient * multiply(sines, imag_now)
            if final_pass:
                imag_next = None
            else:
                imag_next = multiply(cosines, imag_now) + orient * multiply(sines, real_now)
        real_now = rotate(real_next, extent_mid, extent_low)
        imag_now = None if imag_next is None else rotate(imag_next, extent_mid, extent_low)
    return (real_now, imag_now)


def collide(heavy_block, fourier_scattering_table):
    species_count, x_extent_size, cell_count, merged = heavy_block.shape
    flattened = jnp.transpose(heavy_block, (0, 2, 1, 3)).reshape(
        species_count * cell_count, x_extent_size, merged
    )
    spec_real, spec_imag = spectral(flattened, None, -1, False)

    def invert(kernel_index):
        kernel = fourier_scattering_table[kernel_index][None, :, :]
        real_out, unused = spectral(spec_real * kernel, spec_imag * kernel, 1, True)
        return real_out / (NVX * NVY * NVZ)

    gain_sum = invert(0) * invert(1)
    loss_term = flattened * invert(2 * PAIRS)
    updated = flattened + COLLIDE_SCALE * (gain_sum - loss_term)
    return jnp.transpose(
        updated.reshape(species_count, cell_count, x_extent_size, merged), (0, 2, 1, 3)
    )


def split_bf16(values):
    rounded = lax.reduce_precision(values, exponent_bits=8, mantissa_bits=7)
    return rounded.astype(jnp.bfloat16), (values - rounded).astype(jnp.bfloat16)


def kron_tables(extent):
    size = extent * extent
    index = np.arange(size)
    phases = (
        np.outer(index // extent, index // extent) + np.outer(index % extent, index % extent)
    ) % extent
    angles = phases * (2.0 * np.pi / extent)

    def split(values):
        high = values.astype(jnp.bfloat16)
        low = (values - high.astype(np.float64)).astype(jnp.bfloat16)
        return jnp.asarray(high), jnp.asarray(low)

    return split(np.cos(angles)), split(np.sin(angles))


def split_dot(operand, table):
    high, low = table
    op_high, op_low = split_bf16(operand)

    def dot(left, right):
        return jnp.dot(left, right, preferred_element_type=jnp.float32)

    count = operand.shape[0]
    by_high = dot(jnp.concatenate([op_high, op_low], axis=0), high)
    return by_high[:count] + (by_high[count:] + dot(op_high, low))


def collide_kron(heavy_block, fourier_scattering_table):
    species_count, x_extent_size, cell_count, merged = heavy_block.shape
    hp = lax.Precision.HIGHEST
    flat = jnp.transpose(heavy_block, (0, 2, 1, 3)).reshape(
        species_count * cell_count, x_extent_size, merged
    )
    plain = jnp.arange(x_extent_size, dtype=jnp.int32)
    x_cos, x_sin = tables(plain, velocity_index(plain, x_extent_size), x_extent_size)
    wide_cos, wide_sin = kron_tables(NVY)
    rows = species_count * cell_count
    x_real = jnp.einsum("kp,bpm->kbm", x_cos, flat, precision=hp)
    x_imag = -jnp.einsum("kp,bpm->kbm", x_sin, flat, precision=hp)
    stacked = jnp.concatenate([x_real, x_imag], axis=1).reshape(-1, merged)
    by_cos = split_dot(stacked, wide_cos).reshape(x_extent_size, 2, rows, merged)
    by_sin = split_dot(stacked, wide_sin).reshape(x_extent_size, 2, rows, merged)
    spec_real = by_cos[:, 0] + by_sin[:, 1]
    spec_imag = by_cos[:, 1] - by_sin[:, 0]
    kernels = jnp.transpose(fourier_scattering_table, (1, 0, 2))[:, :, None, :]
    z_real = kernels * spec_real[:, None]
    z_imag = kernels * spec_imag[:, None]
    u_real = jnp.einsum("kp,kqbm->pqbm", x_cos, z_real, precision=hp) - jnp.einsum(
        "kp,kqbm->pqbm", x_sin, z_imag, precision=hp
    )
    u_imag = jnp.einsum("kp,kqbm->pqbm", x_sin, z_real, precision=hp) + jnp.einsum(
        "kp,kqbm->pqbm", x_cos, z_imag, precision=hp
    )
    parts = (
        split_dot(u_real.reshape(-1, merged), wide_cos)
        - split_dot(u_imag.reshape(-1, merged), wide_sin)
    ).reshape(
        x_extent_size, fourier_scattering_table.shape[0], rows, merged
    ) / (NVX * NVY * NVZ)
    fields = jnp.transpose(flat, (1, 0, 2))
    updated = fields + COLLIDE_SCALE * (parts[:, 0] * parts[:, 1] - fields * parts[:, 2])
    return jnp.transpose(
        updated.reshape(x_extent_size, species_count, cell_count, merged), (1, 0, 2, 3)
    )


def advance(padded, mirror, odd_stiffness_factor, leading_plane, x_extent_size):
    planes = padded.shape[1]
    positions = leading_plane + jnp.arange(planes, dtype=jnp.int32)
    speeds = plane_speed(velocity_index(positions, x_extent_size), x_extent_size)[
        None, :, None, None
    ]
    even_part = 0.5 * (padded + mirror)
    odd_part = 0.5 * (padded - mirror)
    even_diff = 0.5 * (even_part[:, :, 2:] - even_part[:, :, :-2])
    odd_diff = 0.5 * (odd_part[:, :, 2:] - odd_part[:, :, :-2])
    even_new = even_part[:, :, 1:-1] - speeds * odd_diff
    odd_new = (odd_part[:, :, 1:-1] - speeds * even_diff) / (1.0 + odd_stiffness_factor)[
        :, None, None, None
    ]
    return even_new + odd_new


def moments(light_portion, leading_plane, x_extent_size):
    planes = light_portion.shape[1]
    positions = leading_plane + jnp.arange(planes, dtype=jnp.int32)
    along_first = velocity_values(velocity_index(positions, x_extent_size), x_extent_size)
    along_second = jnp.repeat(velocity_values(jnp.arange(NVY, dtype=jnp.int32), NVY), NVZ)
    along_third = jnp.tile(velocity_values(jnp.arange(NVZ, dtype=jnp.int32), NVZ), NVY)
    density = jnp.sum(light_portion, axis=(1, 3))
    moment_first = jnp.sum(light_portion * along_first[None, :, None, None], axis=(1, 3))
    moment_second = jnp.sum(light_portion * along_second, axis=(1, 3))
    moment_third = jnp.sum(light_portion * along_third, axis=(1, 3))
    return jnp.stack([density, moment_first, moment_second, moment_third])


def relax_light_species(
    light_portion,
    summed_moments,
    leading_plane,
    x_extent_size,
    electron_bgk_frequency_dt,
    electron_kinetic_heat_level,
):
    light_count, planes, cell_count, merged = light_portion.shape
    density = summed_moments[0]
    drifts = summed_moments[1:] / density[None]
    equilibrium_heat_level = electron_kinetic_heat_level[:, None, None]

    def integration_coefficient(values, drift):
        offset_counts_per_row = values[None, None, :] - drift[:, :, None]
        return jnp.exp(
            -(offset_counts_per_row * offset_counts_per_row) / (2.0 * equilibrium_heat_level)
        )

    def profile(values, drift):
        weights = integration_coefficient(values, drift)
        return weights / jnp.sum(weights, axis=2, keepdims=True)

    full_first = integration_coefficient(
        velocity_values(jnp.arange(x_extent_size, dtype=jnp.int32), x_extent_size), drifts[0]
    )
    positions = leading_plane + jnp.arange(planes, dtype=jnp.int32)
    local_values = velocity_values(velocity_index(positions, x_extent_size), x_extent_size)
    local_first = integration_coefficient(local_values, drifts[0]) / jnp.sum(
        full_first, axis=2, keepdims=True
    )
    grid_second = velocity_values(jnp.arange(NVY, dtype=jnp.int32), NVY)
    grid_third = velocity_values(jnp.arange(NVZ, dtype=jnp.int32), NVZ)
    profile_rest = (
        profile(grid_second, drifts[1])[:, :, :, None]
        * profile(grid_third, drifts[2])[:, :, None, :]
    ).reshape(light_count, cell_count, merged)
    maxwell = (
        density[:, None, :, None]
        * jnp.transpose(local_first, (0, 2, 1))[:, :, :, None]
        * profile_rest[:, None, :, :]
    )
    rates = electron_bgk_frequency_dt[:, None, None, None]
    return (light_portion + rates * maxwell) / (1.0 + rates)


def body(
    phase_density_field,
    fourier_scattering_table,
    odd_stiffness_factor,
    electron_bgk_frequency_dt,
    electron_kinetic_heat_level,
):
    species_count = phase_density_field.shape[0]
    heavy_count = species_count - electron_bgk_frequency_dt.shape[0]
    x_extent_size = fourier_scattering_table.shape[1]
    planes = phase_density_field.shape[1]
    padded = extended(phase_density_field, (("space", 2),), 1)
    leading_plane = lax.axis_index("vel") * planes
    positions = leading_plane + jnp.arange(planes, dtype=jnp.int32)
    speeds = plane_speed(velocity_index(positions, x_extent_size), x_extent_size)[
        None, :, None, None
    ]
    shifted = phase_density_field - speeds * (
        0.5 * (padded[:, :, 2:] - padded[:, :, :-2])
    )
    gathered = lax.all_to_all(shifted, "vel", split_axis=2, concat_axis=1, tiled=True)
    half = x_extent_size // 2
    mirror = jnp.flip(
        jnp.concatenate([gathered[:, half:], gathered[:, :half]], axis=1), axis=3
    )
    ratio = 1.0 / (1.0 + odd_stiffness_factor)
    alpha = (0.5 * (1.0 + ratio))[:, None, None, None]
    beta = (0.5 * (1.0 - ratio))[:, None, None, None]
    advanced = alpha * gathered + beta * mirror
    heavy_part = collide_kron(advanced[:heavy_count], fourier_scattering_table)
    light_portion = advanced[heavy_count:]
    summed_moments = moments(light_portion, 0, x_extent_size)
    light_portion = relax_light_species(
        light_portion,
        summed_moments,
        0,
        x_extent_size,
        electron_bgk_frequency_dt,
        electron_kinetic_heat_level,
    )
    result = jnp.concatenate([heavy_part, light_portion], axis=0)
    return lax.all_to_all(result, "vel", split_axis=1, concat_axis=2, tiled=True)


def solution(mesh):
    in_specs = (P(None, "vel", "space", None), P(), P(), P(), P())
    out_specs = P(None, "vel", "space", None)
    return jax.shard_map(body, mesh=mesh, in_specs=in_specs, out_specs=out_specs, check_vma=False)
```

```python
import math

import numpy as np

import jax
import jax.numpy as jnp
from jax import lax
from jax.sharding import PartitionSpec as P

NVX = 32
NVY = 32
NVZ = 32
PAIRS = 1


CFL_NUMBER = 0.2
VELOCITY_STEP = 0.375
COLLIDE_SCALE = 0.25


def extended(x, sides, width):
    for axis, dim in sides:
        devices, length = (lax.axis_size(axis), x.shape[dim])
        up = [(i, (i + 1) % devices) for i in range(devices)]
        down = [(j, i) for i, j in up]
        last = lax.slice_in_dim(x, length - width, length, axis=dim)
        initial = lax.slice_in_dim(x, 0, width, axis=dim)
        before = lax.ppermute(last, axis, up)
        after = lax.ppermute(initial, axis, down)
        x = jnp.concatenate([before, x, after], axis=dim)
    return x


def from_partner(value, axis, stride):
    mask = 2**stride
    pairs = [(source, source ^ mask) for source in range(lax.axis_size(axis))]
    return lax.ppermute(value, axis, pairs)


def velocity_values(indices, extent):
    return (indices.astype(jnp.float32) - (extent - 1) / 2.0) * VELOCITY_STEP


def plane_speed(indices, extent):
    return CFL_NUMBER * (2 * indices - (extent - 1)).astype(jnp.float32) / (extent - 1)


def velocity_index(positions, extent):
    half = extent // 2
    return jnp.where(positions < half, positions, 3 * half - 1 - positions)


def tables(row_index, col_index, extent):
    phases = row_index[:, None] * col_index[None, :] % extent
    angles = phases.astype(jnp.float32) * (2.0 * math.pi / extent)
    return (jnp.cos(angles), jnp.sin(angles))


def multiply(table, operand):
    return jnp.einsum("ka,bam->bkm", table, operand, precision=lax.Precision.HIGHEST)


def rotate(operand, extent_mid, extent_low):
    batch_count, extent_top, merged = operand.shape
    shaped = operand.reshape(batch_count, extent_top, extent_mid, extent_low)
    return jnp.transpose(shaped, (0, 2, 3, 1)).reshape(
        batch_count, extent_mid, extent_low * extent_top
    )


def spectral(real_in, imag_in, orient, real_only):
    extents = (NVX, NVY, NVZ)
    real_now = real_in
    imag_now = imag_in
    for pass_index in range(3):
        extent = extents[pass_index]
        extent_mid = extents[(pass_index + 1) % 3]
        extent_low = extents[(pass_index + 2) % 3]
        plain = jnp.arange(extent, dtype=jnp.int32)
        if pass_index == 0 and orient < 0:
            cosines, sines = tables(plain, velocity_index(plain, extent), extent)
        elif pass_index == 0:
            cosines, sines = tables(velocity_index(plain, extent), plain, extent)
        else:
            cosines, sines = tables(plain, plain, extent)
        final_pass = real_only and pass_index == 2
        if imag_now is None:
            real_next = multiply(cosines, real_now)
            imag_next = orient * multiply(sines, real_now)
        else:
            real_next = multiply(cosines, real_now) - orient * multiply(sines, imag_now)
            if final_pass:
                imag_next = None
            else:
                imag_next = multiply(cosines, imag_now) + orient * multiply(sines, real_now)
        real_now = rotate(real_next, extent_mid, extent_low)
        imag_now = None if imag_next is None else rotate(imag_next, extent_mid, extent_low)
    return (real_now, imag_now)


def collide(heavy_block, fourier_scattering_table):
    species_count, x_extent_size, cell_count, merged = heavy_block.shape
    flattened = jnp.transpose(heavy_block, (0, 2, 1, 3)).reshape(
        species_count * cell_count, x_extent_size, merged
    )
    spec_real, spec_imag = spectral(flattened, None, -1, False)

    def invert(kernel_index):
        kernel = fourier_scattering_table[kernel_index][None, :, :]
        real_out, unused = spectral(spec_real * kernel, spec_imag * kernel, 1, True)
        return real_out / (NVX * NVY * NVZ)

    gain_sum = invert(0) * invert(1)
    loss_term = flattened * invert(2 * PAIRS)
    updated = flattened + COLLIDE_SCALE * (gain_sum - loss_term)
    return jnp.transpose(
        updated.reshape(species_count, cell_count, x_extent_size, merged), (0, 2, 1, 3)
    )


def split_bf16(values):
    rounded = lax.reduce_precision(values, exponent_bits=8, mantissa_bits=7)
    return rounded.astype(jnp.bfloat16), (values - rounded).astype(jnp.bfloat16)


def kron_tables(extent):
    size = extent * extent
    index = np.arange(size)
    phases = (
        np.outer(index // extent, index // extent) + np.outer(index % extent, index % extent)
    ) % extent
    angles = phases * (2.0 * np.pi / extent)

    def split(values):
        high = values.astype(jnp.bfloat16)
        low = (values - high.astype(np.float64)).astype(jnp.bfloat16)
        return jnp.asarray(high), jnp.asarray(low)

    return split(np.cos(angles)), split(np.sin(angles))


def split_dot(operand, table):
    high, low = table
    op_high, op_low = split_bf16(operand)

    def dot(left, right):
        return jnp.dot(left, right, preferred_element_type=jnp.float32)

    return dot(op_high, high) + (dot(op_low, high) + dot(op_high, low))


def collide_kron(heavy_block, fourier_scattering_table):
    species_count, x_extent_size, cell_count, merged = heavy_block.shape
    hp = lax.Precision.HIGHEST
    flat = jnp.transpose(heavy_block, (0, 2, 1, 3)).reshape(
        species_count * cell_count, x_extent_size, merged
    )
    plain = jnp.arange(x_extent_size, dtype=jnp.int32)
    x_cos, x_sin = tables(plain, velocity_index(plain, x_extent_size), x_extent_size)
    wide_cos, wide_sin = kron_tables(NVY)
    rows = species_count * cell_count
    x_real = jnp.einsum("kp,bpm->kbm", x_cos, flat, precision=hp)
    x_imag = -jnp.einsum("kp,bpm->kbm", x_sin, flat, precision=hp)
    stacked = jnp.concatenate([x_real, x_imag], axis=1).reshape(-1, merged)
    by_cos = split_dot(stacked, wide_cos).reshape(x_extent_size, 2, rows, merged)
    by_sin = split_dot(stacked, wide_sin).reshape(x_extent_size, 2, rows, merged)
    spec_real = by_cos[:, 0] + by_sin[:, 1]
    spec_imag = by_cos[:, 1] - by_sin[:, 0]
    kernels = jnp.transpose(fourier_scattering_table, (1, 0, 2))[:, :, None, :]
    z_real = kernels * spec_real[:, None]
    z_imag = kernels * spec_imag[:, None]
    u_real = jnp.einsum("kp,kqbm->pqbm", x_cos, z_real, precision=hp) - jnp.einsum(
        "kp,kqbm->pqbm", x_sin, z_imag, precision=hp
    )
    u_imag = jnp.einsum("kp,kqbm->pqbm", x_sin, z_real, precision=hp) + jnp.einsum(
        "kp,kqbm->pqbm", x_cos, z_imag, precision=hp
    )
    parts = (
        split_dot(u_real.reshape(-1, merged), wide_cos)
        - split_dot(u_imag.reshape(-1, merged), wide_sin)
    ).reshape(
        x_extent_size, fourier_scattering_table.shape[0], rows, merged
    ) / (NVX * NVY * NVZ)
    fields = jnp.transpose(flat, (1, 0, 2))
    updated = fields + COLLIDE_SCALE * (parts[:, 0] * parts[:, 1] - fields * parts[:, 2])
    return jnp.transpose(
        updated.reshape(x_extent_size, species_count, cell_count, merged), (1, 0, 2, 3)
    )


def advance(padded, mirror, odd_stiffness_factor, leading_plane, x_extent_size):
    planes = padded.shape[1]
    positions = leading_plane + jnp.arange(planes, dtype=jnp.int32)
    speeds = plane_speed(velocity_index(positions, x_extent_size), x_extent_size)[
        None, :, None, None
    ]
    even_part = 0.5 * (padded + mirror)
    odd_part = 0.5 * (padded - mirror)
    even_diff = 0.5 * (even_part[:, :, 2:] - even_part[:, :, :-2])
    odd_diff = 0.5 * (odd_part[:, :, 2:] - odd_part[:, :, :-2])
    even_new = even_part[:, :, 1:-1] - speeds * odd_diff
    odd_new = (odd_part[:, :, 1:-1] - speeds * even_diff) / (1.0 + odd_stiffness_factor)[
        :, None, None, None
    ]
    return even_new + odd_new


def moments(light_portion, leading_plane, x_extent_size):
    planes = light_portion.shape[1]
    positions = leading_plane + jnp.arange(planes, dtype=jnp.int32)
    along_first = velocity_values(velocity_index(positions, x_extent_size), x_extent_size)
    along_second = jnp.repeat(velocity_values(jnp.arange(NVY, dtype=jnp.int32), NVY), NVZ)
    along_third = jnp.tile(velocity_values(jnp.arange(NVZ, dtype=jnp.int32), NVZ), NVY)
    density = jnp.sum(light_portion, axis=(1, 3))
    moment_first = jnp.sum(light_portion * along_first[None, :, None, None], axis=(1, 3))
    moment_second = jnp.sum(light_portion * along_second, axis=(1, 3))
    moment_third = jnp.sum(light_portion * along_third, axis=(1, 3))
    return jnp.stack([density, moment_first, moment_second, moment_third])


def relax_light_species(
    light_portion,
    summed_moments,
    leading_plane,
    x_extent_size,
    electron_bgk_frequency_dt,
    electron_kinetic_heat_level,
):
    light_count, planes, cell_count, merged = light_portion.shape
    density = summed_moments[0]
    drifts = summed_moments[1:] / density[None]
    equilibrium_heat_level = electron_kinetic_heat_level[:, None, None]

    def integration_coefficient(values, drift):
        offset_counts_per_row = values[None, None, :] - drift[:, :, None]
        return jnp.exp(
            -(offset_counts_per_row * offset_counts_per_row) / (2.0 * equilibrium_heat_level)
        )

    def profile(values, drift):
        weights = integration_coefficient(values, drift)
        return weights / jnp.sum(weights, axis=2, keepdims=True)

    full_first = integration_coefficient(
        velocity_values(jnp.arange(x_extent_size, dtype=jnp.int32), x_extent_size), drifts[0]
    )
    positions = leading_plane + jnp.arange(planes, dtype=jnp.int32)
    local_values = velocity_values(velocity_index(positions, x_extent_size), x_extent_size)
    local_first = integration_coefficient(local_values, drifts[0]) / jnp.sum(
        full_first, axis=2, keepdims=True
    )
    grid_second = velocity_values(jnp.arange(NVY, dtype=jnp.int32), NVY)
    grid_third = velocity_values(jnp.arange(NVZ, dtype=jnp.int32), NVZ)
    profile_rest = (
        profile(grid_second, drifts[1])[:, :, :, None]
        * profile(grid_third, drifts[2])[:, :, None, :]
    ).reshape(light_count, cell_count, merged)
    maxwell = (
        density[:, None, :, None]
        * jnp.transpose(local_first, (0, 2, 1))[:, :, :, None]
        * profile_rest[:, None, :, :]
    )
    rates = electron_bgk_frequency_dt[:, None, None, None]
    return (light_portion + rates * maxwell) / (1.0 + rates)


def body(
    phase_density_field,
    fourier_scattering_table,
    odd_stiffness_factor,
    electron_bgk_frequency_dt,
    electron_kinetic_heat_level,
):
    species_count = phase_density_field.shape[0]
    heavy_count = species_count - electron_bgk_frequency_dt.shape[0]
    x_extent_size = fourier_scattering_table.shape[1]
    planes = phase_density_field.shape[1]
    padded = extended(phase_density_field, (("space", 2),), 1)
    leading_plane = lax.axis_index("vel") * planes
    positions = leading_plane + jnp.arange(planes, dtype=jnp.int32)
    speeds = plane_speed(velocity_index(positions, x_extent_size), x_extent_size)[
        None, :, None, None
    ]
    shifted = phase_density_field - speeds * (
        0.5 * (padded[:, :, 2:] - padded[:, :, :-2])
    )
    half = x_extent_size // 2
    ratio = 1.0 / (1.0 + odd_stiffness_factor)
    alpha = (0.5 * (1.0 + ratio))[:, None, None, None]
    beta = (0.5 * (1.0 - ratio))[:, None, None, None]

    def gather_advance(first, last):
        gathered = lax.all_to_all(
            shifted[first:last], "vel", split_axis=2, concat_axis=1, tiled=True
        )
        mirror = jnp.flip(
            jnp.concatenate([gathered[:, half:], gathered[:, :half]], axis=1), axis=3
        )
        return alpha[first:last] * gathered + beta[first:last] * mirror

    light_portion = gather_advance(heavy_count, species_count)
    summed_moments = moments(light_portion, 0, x_extent_size)
    light_portion = relax_light_species(
        light_portion,
        summed_moments,
        0,
        x_extent_size,
        electron_bgk_frequency_dt,
        electron_kinetic_heat_level,
    )
    light_back = lax.all_to_all(light_portion, "vel", split_axis=1, concat_axis=2, tiled=True)
    heavy_part = collide_kron(gather_advance(0, heavy_count), fourier_scattering_table)
    heavy_back = lax.all_to_all(heavy_part, "vel", split_axis=1, concat_axis=2, tiled=True)
    return jnp.concatenate([heavy_back, light_back], axis=0)


def solution(mesh):
    in_specs = (P(None, "vel", "space", None), P(), P(), P(), P())
    out_specs = P(None, "vel", "space", None)
    return jax.shard_map(body, mesh=mesh, in_specs=in_specs, out_specs=out_specs, check_vma=False)
```

```python
import math

import numpy as np

import jax
import jax.numpy as jnp
from jax import lax
from jax.sharding import PartitionSpec as P

NVX = 32
NVY = 32
NVZ = 32
PAIRS = 1


CFL_NUMBER = 0.2
VELOCITY_STEP = 0.375
COLLIDE_SCALE = 0.25


def extended(x, sides, width):
    for axis, dim in sides:
        devices, length = (lax.axis_size(axis), x.shape[dim])
        up = [(i, (i + 1) % devices) for i in range(devices)]
        down = [(j, i) for i, j in up]
        last = lax.slice_in_dim(x, length - width, length, axis=dim)
        initial = lax.slice_in_dim(x, 0, width, axis=dim)
        before = lax.ppermute(last, axis, up)
        after = lax.ppermute(initial, axis, down)
        x = jnp.concatenate([before, x, after], axis=dim)
    return x


def from_partner(value, axis, stride):
    mask = 2**stride
    pairs = [(source, source ^ mask) for source in range(lax.axis_size(axis))]
    return lax.ppermute(value, axis, pairs)


def velocity_values(indices, extent):
    return (indices.astype(jnp.float32) - (extent - 1) / 2.0) * VELOCITY_STEP


def plane_speed(indices, extent):
    return CFL_NUMBER * (2 * indices - (extent - 1)).astype(jnp.float32) / (extent - 1)


def velocity_index(positions, extent):
    half = extent // 2
    return jnp.where(positions < half, positions, 3 * half - 1 - positions)


def tables(row_index, col_index, extent):
    phases = row_index[:, None] * col_index[None, :] % extent
    angles = phases.astype(jnp.float32) * (2.0 * math.pi / extent)
    return (jnp.cos(angles), jnp.sin(angles))


def multiply(table, operand):
    return jnp.einsum("ka,bam->bkm", table, operand, precision=lax.Precision.HIGHEST)


def rotate(operand, extent_mid, extent_low):
    batch_count, extent_top, merged = operand.shape
    shaped = operand.reshape(batch_count, extent_top, extent_mid, extent_low)
    return jnp.transpose(shaped, (0, 2, 3, 1)).reshape(
        batch_count, extent_mid, extent_low * extent_top
    )


def spectral(real_in, imag_in, orient, real_only):
    extents = (NVX, NVY, NVZ)
    real_now = real_in
    imag_now = imag_in
    for pass_index in range(3):
        extent = extents[pass_index]
        extent_mid = extents[(pass_index + 1) % 3]
        extent_low = extents[(pass_index + 2) % 3]
        plain = jnp.arange(extent, dtype=jnp.int32)
        if pass_index == 0 and orient < 0:
            cosines, sines = tables(plain, velocity_index(plain, extent), extent)
        elif pass_index == 0:
            cosines, sines = tables(velocity_index(plain, extent), plain, extent)
        else:
            cosines, sines = tables(plain, plain, extent)
        final_pass = real_only and pass_index == 2
        if imag_now is None:
            real_next = multiply(cosines, real_now)
            imag_next = orient * multiply(sines, real_now)
        else:
            real_next = multiply(cosines, real_now) - orient * multiply(sines, imag_now)
            if final_pass:
                imag_next = None
            else:
                imag_next = multiply(cosines, imag_now) + orient * multiply(sines, real_now)
        real_now = rotate(real_next, extent_mid, extent_low)
        imag_now = None if imag_next is None else rotate(imag_next, extent_mid, extent_low)
    return (real_now, imag_now)


def collide(heavy_block, fourier_scattering_table):
    species_count, x_extent_size, cell_count, merged = heavy_block.shape
    flattened = jnp.transpose(heavy_block, (0, 2, 1, 3)).reshape(
        species_count * cell_count, x_extent_size, merged
    )
    spec_real, spec_imag = spectral(flattened, None, -1, False)

    def invert(kernel_index):
        kernel = fourier_scattering_table[kernel_index][None, :, :]
        real_out, unused = spectral(spec_real * kernel, spec_imag * kernel, 1, True)
        return real_out / (NVX * NVY * NVZ)

    gain_sum = invert(0) * invert(1)
    loss_term = flattened * invert(2 * PAIRS)
    updated = flattened + COLLIDE_SCALE * (gain_sum - loss_term)
    return jnp.transpose(
        updated.reshape(species_count, cell_count, x_extent_size, merged), (0, 2, 1, 3)
    )


def split_bf16(values):
    rounded = lax.reduce_precision(values, exponent_bits=8, mantissa_bits=7)
    return rounded.astype(jnp.bfloat16), (values - rounded).astype(jnp.bfloat16)


def kron_tables(extent):
    size = extent * extent
    index = np.arange(size)
    phases = (
        np.outer(index // extent, index // extent) + np.outer(index % extent, index % extent)
    ) % extent
    angles = phases * (2.0 * np.pi / extent)

    def split(values):
        high = values.astype(jnp.bfloat16)
        low = (values - high.astype(np.float64)).astype(jnp.bfloat16)
        return jnp.asarray(high), jnp.asarray(low)

    return split(np.cos(angles)), split(np.sin(angles))


def split_dot(operand, table):
    high, low = table
    op_high, op_low = split_bf16(operand)

    def dot(left, right):
        return jnp.dot(left, right, preferred_element_type=jnp.float32)

    return dot(op_high, high) + (dot(op_low, high) + dot(op_high, low))


def collide_kron(heavy_block, fourier_scattering_table):
    species_count, x_extent_size, cell_count, merged = heavy_block.shape
    hp = lax.Precision.HIGHEST
    flat = jnp.transpose(heavy_block, (0, 2, 1, 3)).reshape(
        species_count * cell_count, x_extent_size, merged
    )
    rows = species_count * cell_count
    kernel_count = fourier_scattering_table.shape[0]
    plain = jnp.arange(x_extent_size, dtype=jnp.int32)
    x_cos, x_sin = tables(plain, velocity_index(plain, x_extent_size), x_extent_size)
    wide_cos, wide_sin = kron_tables(NVY)
    square = (x_extent_size, x_extent_size)
    fwd_cos = jnp.broadcast_to(x_cos, (rows,) + square)
    fwd_sin = jnp.broadcast_to(x_sin, (rows,) + square)
    x_real = jnp.einsum("bkp,bpm->bkm", fwd_cos, flat, precision=hp)
    x_imag = -jnp.einsum("bkp,bpm->bkm", fwd_sin, flat, precision=hp)
    stacked = jnp.concatenate([x_real, x_imag], axis=0).reshape(-1, merged)
    by_cos = split_dot(stacked, wide_cos).reshape(2, rows, x_extent_size, merged)
    by_sin = split_dot(stacked, wide_sin).reshape(2, rows, x_extent_size, merged)
    spec_real = by_cos[0] + by_sin[1]
    spec_imag = by_cos[1] - by_sin[0]
    kernels = fourier_scattering_table[:, None]
    z_real = kernels * spec_real[None]
    z_imag = kernels * spec_imag[None]
    inv_cos = jnp.broadcast_to(x_cos.T, (kernel_count, rows) + square)
    inv_sin = jnp.broadcast_to(x_sin.T, (kernel_count, rows) + square)
    u_real = jnp.einsum("qbpk,qbkm->qbpm", inv_cos, z_real, precision=hp) - jnp.einsum(
        "qbpk,qbkm->qbpm", inv_sin, z_imag, precision=hp
    )
    u_imag = jnp.einsum("qbpk,qbkm->qbpm", inv_sin, z_real, precision=hp) + jnp.einsum(
        "qbpk,qbkm->qbpm", inv_cos, z_imag, precision=hp
    )
    parts = (
        split_dot(u_real.reshape(-1, merged), wide_cos)
        - split_dot(u_imag.reshape(-1, merged), wide_sin)
    ).reshape(kernel_count, rows, x_extent_size, merged) / (NVX * NVY * NVZ)
    updated = flat + COLLIDE_SCALE * (parts[0] * parts[1] - flat * parts[2])
    return jnp.transpose(
        updated.reshape(species_count, cell_count, x_extent_size, merged), (0, 2, 1, 3)
    )


def advance(padded, mirror, odd_stiffness_factor, leading_plane, x_extent_size):
    planes = padded.shape[1]
    positions = leading_plane + jnp.arange(planes, dtype=jnp.int32)
    speeds = plane_speed(velocity_index(positions, x_extent_size), x_extent_size)[
        None, :, None, None
    ]
    even_part = 0.5 * (padded + mirror)
    odd_part = 0.5 * (padded - mirror)
    even_diff = 0.5 * (even_part[:, :, 2:] - even_part[:, :, :-2])
    odd_diff = 0.5 * (odd_part[:, :, 2:] - odd_part[:, :, :-2])
    even_new = even_part[:, :, 1:-1] - speeds * odd_diff
    odd_new = (odd_part[:, :, 1:-1] - speeds * even_diff) / (1.0 + odd_stiffness_factor)[
        :, None, None, None
    ]
    return even_new + odd_new


def moments(light_portion, leading_plane, x_extent_size):
    planes = light_portion.shape[1]
    positions = leading_plane + jnp.arange(planes, dtype=jnp.int32)
    along_first = velocity_values(velocity_index(positions, x_extent_size), x_extent_size)
    along_second = jnp.repeat(velocity_values(jnp.arange(NVY, dtype=jnp.int32), NVY), NVZ)
    along_third = jnp.tile(velocity_values(jnp.arange(NVZ, dtype=jnp.int32), NVZ), NVY)
    density = jnp.sum(light_portion, axis=(1, 3))
    moment_first = jnp.sum(light_portion * along_first[None, :, None, None], axis=(1, 3))
    moment_second = jnp.sum(light_portion * along_second, axis=(1, 3))
    moment_third = jnp.sum(light_portion * along_third, axis=(1, 3))
    return jnp.stack([density, moment_first, moment_second, moment_third])


def relax_light_species(
    light_portion,
    summed_moments,
    leading_plane,
    x_extent_size,
    electron_bgk_frequency_dt,
    electron_kinetic_heat_level,
):
    light_count, planes, cell_count, merged = light_portion.shape
    density = summed_moments[0]
    drifts = summed_moments[1:] / density[None]
    equilibrium_heat_level = electron_kinetic_heat_level[:, None, None]

    def integration_coefficient(values, drift):
        offset_counts_per_row = values[None, None, :] - drift[:, :, None]
        return jnp.exp(
            -(offset_counts_per_row * offset_counts_per_row) / (2.0 * equilibrium_heat_level)
        )

    def profile(values, drift):
        weights = integration_coefficient(values, drift)
        return weights / jnp.sum(weights, axis=2, keepdims=True)

    full_first = integration_coefficient(
        velocity_values(jnp.arange(x_extent_size, dtype=jnp.int32), x_extent_size), drifts[0]
    )
    positions = leading_plane + jnp.arange(planes, dtype=jnp.int32)
    local_values = velocity_values(velocity_index(positions, x_extent_size), x_extent_size)
    local_first = integration_coefficient(local_values, drifts[0]) / jnp.sum(
        full_first, axis=2, keepdims=True
    )
    grid_second = velocity_values(jnp.arange(NVY, dtype=jnp.int32), NVY)
    grid_third = velocity_values(jnp.arange(NVZ, dtype=jnp.int32), NVZ)
    profile_rest = (
        profile(grid_second, drifts[1])[:, :, :, None]
        * profile(grid_third, drifts[2])[:, :, None, :]
    ).reshape(light_count, cell_count, merged)
    maxwell = (
        density[:, None, :, None]
        * jnp.transpose(local_first, (0, 2, 1))[:, :, :, None]
        * profile_rest[:, None, :, :]
    )
    rates = electron_bgk_frequency_dt[:, None, None, None]
    return (light_portion + rates * maxwell) / (1.0 + rates)


def body(
    phase_density_field,
    fourier_scattering_table,
    odd_stiffness_factor,
    electron_bgk_frequency_dt,
    electron_kinetic_heat_level,
):
    species_count = phase_density_field.shape[0]
    heavy_count = species_count - electron_bgk_frequency_dt.shape[0]
    x_extent_size = fourier_scattering_table.shape[1]
    planes = phase_density_field.shape[1]
    padded = extended(phase_density_field, (("space", 2),), 1)
    leading_plane = lax.axis_index("vel") * planes
    positions = leading_plane + jnp.arange(planes, dtype=jnp.int32)
    speeds = plane_speed(velocity_index(positions, x_extent_size), x_extent_size)[
        None, :, None, None
    ]
    shifted = phase_density_field - speeds * (
        0.5 * (padded[:, :, 2:] - padded[:, :, :-2])
    )
    gathered = lax.all_to_all(shifted, "vel", split_axis=2, concat_axis=1, tiled=True)
    half = x_extent_size // 2
    mirror = jnp.flip(
        jnp.concatenate([gathered[:, half:], gathered[:, :half]], axis=1), axis=3
    )
    ratio = 1.0 / (1.0 + odd_stiffness_factor)
    alpha = (0.5 * (1.0 + ratio))[:, None, None, None]
    beta = (0.5 * (1.0 - ratio))[:, None, None, None]
    advanced = alpha * gathered + beta * mirror
    heavy_part = collide_kron(advanced[:heavy_count], fourier_scattering_table)
    light_portion = advanced[heavy_count:]
    summed_moments = moments(light_portion, 0, x_extent_size)
    light_portion = relax_light_species(
        light_portion,
        summed_moments,
        0,
        x_extent_size,
        electron_bgk_frequency_dt,
        electron_kinetic_heat_level,
    )
    result = jnp.concatenate([heavy_part, light_portion], axis=0)
    return lax.all_to_all(result, "vel", split_axis=1, concat_axis=2, tiled=True)


def solution(mesh):
    in_specs = (P(None, "vel", "space", None), P(), P(), P(), P())
    out_specs = P(None, "vel", "space", None)
    return jax.shard_map(body, mesh=mesh, in_specs=in_specs, out_specs=out_specs, check_vma=False)
```

```python
import math

import numpy as np

import jax
import jax.numpy as jnp
from jax import lax
from jax.sharding import PartitionSpec as P

NVX = 32
NVY = 32
NVZ = 32
PAIRS = 1


CFL_NUMBER = 0.2
VELOCITY_STEP = 0.375
COLLIDE_SCALE = 0.25


def extended(x, sides, width):
    for axis, dim in sides:
        devices, length = (lax.axis_size(axis), x.shape[dim])
        up = [(i, (i + 1) % devices) for i in range(devices)]
        down = [(j, i) for i, j in up]
        last = lax.slice_in_dim(x, length - width, length, axis=dim)
        initial = lax.slice_in_dim(x, 0, width, axis=dim)
        before = lax.ppermute(last, axis, up)
        after = lax.ppermute(initial, axis, down)
        x = jnp.concatenate([before, x, after], axis=dim)
    return x


def from_partner(value, axis, stride):
    mask = 2**stride
    pairs = [(source, source ^ mask) for source in range(lax.axis_size(axis))]
    return lax.ppermute(value, axis, pairs)


def velocity_values(indices, extent):
    return (indices.astype(jnp.float32) - (extent - 1) / 2.0) * VELOCITY_STEP


def plane_speed(indices, extent):
    return CFL_NUMBER * (2 * indices - (extent - 1)).astype(jnp.float32) / (extent - 1)


def velocity_index(positions, extent):
    half = extent // 2
    return jnp.where(positions < half, positions, 3 * half - 1 - positions)


def tables(row_index, col_index, extent):
    phases = row_index[:, None] * col_index[None, :] % extent
    angles = phases.astype(jnp.float32) * (2.0 * math.pi / extent)
    return (jnp.cos(angles), jnp.sin(angles))


def multiply(table, operand):
    return jnp.einsum("ka,bam->bkm", table, operand, precision=lax.Precision.HIGHEST)


def rotate(operand, extent_mid, extent_low):
    batch_count, extent_top, merged = operand.shape
    shaped = operand.reshape(batch_count, extent_top, extent_mid, extent_low)
    return jnp.transpose(shaped, (0, 2, 3, 1)).reshape(
        batch_count, extent_mid, extent_low * extent_top
    )


def spectral(real_in, imag_in, orient, real_only):
    extents = (NVX, NVY, NVZ)
    real_now = real_in
    imag_now = imag_in
    for pass_index in range(3):
        extent = extents[pass_index]
        extent_mid = extents[(pass_index + 1) % 3]
        extent_low = extents[(pass_index + 2) % 3]
        plain = jnp.arange(extent, dtype=jnp.int32)
        if pass_index == 0 and orient < 0:
            cosines, sines = tables(plain, velocity_index(plain, extent), extent)
        elif pass_index == 0:
            cosines, sines = tables(velocity_index(plain, extent), plain, extent)
        else:
            cosines, sines = tables(plain, plain, extent)
        final_pass = real_only and pass_index == 2
        if imag_now is None:
            real_next = multiply(cosines, real_now)
            imag_next = orient * multiply(sines, real_now)
        else:
            real_next = multiply(cosines, real_now) - orient * multiply(sines, imag_now)
            if final_pass:
                imag_next = None
            else:
                imag_next = multiply(cosines, imag_now) + orient * multiply(sines, real_now)
        real_now = rotate(real_next, extent_mid, extent_low)
        imag_now = None if imag_next is None else rotate(imag_next, extent_mid, extent_low)
    return (real_now, imag_now)


def collide(heavy_block, fourier_scattering_table):
    species_count, x_extent_size, cell_count, merged = heavy_block.shape
    flattened = jnp.transpose(heavy_block, (0, 2, 1, 3)).reshape(
        species_count * cell_count, x_extent_size, merged
    )
    spec_real, spec_imag = spectral(flattened, None, -1, False)

    def invert(kernel_index):
        kernel = fourier_scattering_table[kernel_index][None, :, :]
        real_out, unused = spectral(spec_real * kernel, spec_imag * kernel, 1, True)
        return real_out / (NVX * NVY * NVZ)

    gain_sum = invert(0) * invert(1)
    loss_term = flattened * invert(2 * PAIRS)
    updated = flattened + COLLIDE_SCALE * (gain_sum - loss_term)
    return jnp.transpose(
        updated.reshape(species_count, cell_count, x_extent_size, merged), (0, 2, 1, 3)
    )


def split_bf16(values):
    rounded = lax.reduce_precision(values, exponent_bits=8, mantissa_bits=7)
    return rounded.astype(jnp.bfloat16), (values - rounded).astype(jnp.bfloat16)


def kron_tables(extent):
    size = extent * extent
    index = np.arange(size)
    phases = (
        np.outer(index // extent, index // extent) + np.outer(index % extent, index % extent)
    ) % extent
    angles = phases * (2.0 * np.pi / extent)

    def split(values):
        high = values.astype(jnp.bfloat16)
        low = (values - high.astype(np.float64)).astype(jnp.bfloat16)
        return jnp.asarray(high), jnp.asarray(low)

    return split(np.cos(angles)), split(np.sin(angles))


def split_dot(operand, table):
    high, low = table
    op_high, op_low = split_bf16(operand)

    def dot(left, right):
        return jnp.dot(left, right, preferred_element_type=jnp.float32)

    return dot(op_high, high) + (dot(op_low, high) + dot(op_high, low))


def collide_kron(heavy_block, fourier_scattering_table):
    species_count, x_extent_size, cell_count, merged = heavy_block.shape
    hp = lax.Precision.HIGHEST
    flat = jnp.transpose(heavy_block, (0, 2, 1, 3)).reshape(
        species_count * cell_count, x_extent_size, merged
    )
    rows = species_count * cell_count
    kernel_count = fourier_scattering_table.shape[0]
    plain = jnp.arange(x_extent_size, dtype=jnp.int32)
    x_cos, x_sin = tables(plain, velocity_index(plain, x_extent_size), x_extent_size)
    wide_cos, wide_sin = kron_tables(NVY)
    square = (x_extent_size, x_extent_size)
    forward = jnp.concatenate([x_cos, -x_sin], axis=0)
    spectrum_x = jnp.einsum(
        "bjp,bpm->bjm", jnp.broadcast_to(forward, (rows,) + forward.shape), flat, precision=hp
    )
    stacked = jnp.transpose(
        spectrum_x.reshape(rows, 2, x_extent_size, merged), (1, 0, 2, 3)
    ).reshape(-1, merged)
    by_cos = split_dot(stacked, wide_cos).reshape(2, rows, x_extent_size, merged)
    by_sin = split_dot(stacked, wide_sin).reshape(2, rows, x_extent_size, merged)
    spec_real = by_cos[0] + by_sin[1]
    spec_imag = by_cos[1] - by_sin[0]
    kernels = fourier_scattering_table[:, None]
    z_both = jnp.concatenate([kernels * spec_real[None], kernels * spec_imag[None]], axis=2)
    inverse = jnp.concatenate(
        [
            jnp.concatenate([x_cos.T, -x_sin.T], axis=1),
            jnp.concatenate([x_sin.T, x_cos.T], axis=1),
        ],
        axis=0,
    )
    u_both = jnp.einsum(
        "qbij,qbjm->qbim",
        jnp.broadcast_to(inverse, (kernel_count, rows) + inverse.shape),
        z_both,
        precision=hp,
    )
    u_real = u_both[:, :, :x_extent_size]
    u_imag = u_both[:, :, x_extent_size:]
    parts = (
        split_dot(u_real.reshape(-1, merged), wide_cos)
        - split_dot(u_imag.reshape(-1, merged), wide_sin)
    ).reshape(kernel_count, rows, x_extent_size, merged) / (NVX * NVY * NVZ)
    updated = flat + COLLIDE_SCALE * (parts[0] * parts[1] - flat * parts[2])
    return jnp.transpose(
        updated.reshape(species_count, cell_count, x_extent_size, merged), (0, 2, 1, 3)
    )


def advance(padded, mirror, odd_stiffness_factor, leading_plane, x_extent_size):
    planes = padded.shape[1]
    positions = leading_plane + jnp.arange(planes, dtype=jnp.int32)
    speeds = plane_speed(velocity_index(positions, x_extent_size), x_extent_size)[
        None, :, None, None
    ]
    even_part = 0.5 * (padded + mirror)
    odd_part = 0.5 * (padded - mirror)
    even_diff = 0.5 * (even_part[:, :, 2:] - even_part[:, :, :-2])
    odd_diff = 0.5 * (odd_part[:, :, 2:] - odd_part[:, :, :-2])
    even_new = even_part[:, :, 1:-1] - speeds * odd_diff
    odd_new = (odd_part[:, :, 1:-1] - speeds * even_diff) / (1.0 + odd_stiffness_factor)[
        :, None, None, None
    ]
    return even_new + odd_new


def moments(light_portion, leading_plane, x_extent_size):
    planes = light_portion.shape[1]
    positions = leading_plane + jnp.arange(planes, dtype=jnp.int32)
    along_first = velocity_values(velocity_index(positions, x_extent_size), x_extent_size)
    along_second = jnp.repeat(velocity_values(jnp.arange(NVY, dtype=jnp.int32), NVY), NVZ)
    along_third = jnp.tile(velocity_values(jnp.arange(NVZ, dtype=jnp.int32), NVZ), NVY)
    density = jnp.sum(light_portion, axis=(1, 3))
    moment_first = jnp.sum(light_portion * along_first[None, :, None, None], axis=(1, 3))
    moment_second = jnp.sum(light_portion * along_second, axis=(1, 3))
    moment_third = jnp.sum(light_portion * along_third, axis=(1, 3))
    return jnp.stack([density, moment_first, moment_second, moment_third])


def relax_light_species(
    light_portion,
    summed_moments,
    leading_plane,
    x_extent_size,
    electron_bgk_frequency_dt,
    electron_kinetic_heat_level,
):
    light_count, planes, cell_count, merged = light_portion.shape
    density = summed_moments[0]
    drifts = summed_moments[1:] / density[None]
    equilibrium_heat_level = electron_kinetic_heat_level[:, None, None]

    def integration_coefficient(values, drift):
        offset_counts_per_row = values[None, None, :] - drift[:, :, None]
        return jnp.exp(
            -(offset_counts_per_row * offset_counts_per_row) / (2.0 * equilibrium_heat_level)
        )

    def profile(values, drift):
        weights = integration_coefficient(values, drift)
        return weights / jnp.sum(weights, axis=2, keepdims=True)

    full_first = integration_coefficient(
        velocity_values(jnp.arange(x_extent_size, dtype=jnp.int32), x_extent_size), drifts[0]
    )
    positions = leading_plane + jnp.arange(planes, dtype=jnp.int32)
    local_values = velocity_values(velocity_index(positions, x_extent_size), x_extent_size)
    local_first = integration_coefficient(local_values, drifts[0]) / jnp.sum(
        full_first, axis=2, keepdims=True
    )
    grid_second = velocity_values(jnp.arange(NVY, dtype=jnp.int32), NVY)
    grid_third = velocity_values(jnp.arange(NVZ, dtype=jnp.int32), NVZ)
    profile_rest = (
        profile(grid_second, drifts[1])[:, :, :, None]
        * profile(grid_third, drifts[2])[:, :, None, :]
    ).reshape(light_count, cell_count, merged)
    maxwell = (
        density[:, None, :, None]
        * jnp.transpose(local_first, (0, 2, 1))[:, :, :, None]
        * profile_rest[:, None, :, :]
    )
    rates = electron_bgk_frequency_dt[:, None, None, None]
    return (light_portion + rates * maxwell) / (1.0 + rates)


def body(
    phase_density_field,
    fourier_scattering_table,
    odd_stiffness_factor,
    electron_bgk_frequency_dt,
    electron_kinetic_heat_level,
):
    species_count = phase_density_field.shape[0]
    heavy_count = species_count - electron_bgk_frequency_dt.shape[0]
    x_extent_size = fourier_scattering_table.shape[1]
    planes = phase_density_field.shape[1]
    padded = extended(phase_density_field, (("space", 2),), 1)
    leading_plane = lax.axis_index("vel") * planes
    positions = leading_plane + jnp.arange(planes, dtype=jnp.int32)
    speeds = plane_speed(velocity_index(positions, x_extent_size), x_extent_size)[
        None, :, None, None
    ]
    shifted = phase_density_field - speeds * (
        0.5 * (padded[:, :, 2:] - padded[:, :, :-2])
    )
    gathered = lax.all_to_all(shifted, "vel", split_axis=2, concat_axis=1, tiled=True)
    half = x_extent_size // 2
    mirror = jnp.flip(
        jnp.concatenate([gathered[:, half:], gathered[:, :half]], axis=1), axis=3
    )
    ratio = 1.0 / (1.0 + odd_stiffness_factor)
    alpha = (0.5 * (1.0 + ratio))[:, None, None, None]
    beta = (0.5 * (1.0 - ratio))[:, None, None, None]
    advanced = alpha * gathered + beta * mirror
    heavy_part = collide_kron(advanced[:heavy_count], fourier_scattering_table)
    light_portion = advanced[heavy_count:]
    summed_moments = moments(light_portion, 0, x_extent_size)
    light_portion = relax_light_species(
        light_portion,
        summed_moments,
        0,
        x_extent_size,
        electron_bgk_frequency_dt,
        electron_kinetic_heat_level,
    )
    result = jnp.concatenate([heavy_part, light_portion], axis=0)
    return lax.all_to_all(result, "vel", split_axis=1, concat_axis=2, tiled=True)


def solution(mesh):
    in_specs = (P(None, "vel", "space", None), P(), P(), P(), P())
    out_specs = P(None, "vel", "space", None)
    return jax.shard_map(body, mesh=mesh, in_specs=in_specs, out_specs=out_specs, check_vma=False)
```

```python
import math

import numpy as np

import jax
import jax.numpy as jnp
from jax import lax
from jax.sharding import PartitionSpec as P

NVX = 32
NVY = 32
NVZ = 32
PAIRS = 1


CFL_NUMBER = 0.2
VELOCITY_STEP = 0.375
COLLIDE_SCALE = 0.25


def extended(x, sides, width):
    for axis, dim in sides:
        devices, length = (lax.axis_size(axis), x.shape[dim])
        up = [(i, (i + 1) % devices) for i in range(devices)]
        down = [(j, i) for i, j in up]
        last = lax.slice_in_dim(x, length - width, length, axis=dim)
        initial = lax.slice_in_dim(x, 0, width, axis=dim)
        before = lax.ppermute(last, axis, up)
        after = lax.ppermute(initial, axis, down)
        x = jnp.concatenate([before, x, after], axis=dim)
    return x


def from_partner(value, axis, stride):
    mask = 2**stride
    pairs = [(source, source ^ mask) for source in range(lax.axis_size(axis))]
    return lax.ppermute(value, axis, pairs)


def velocity_values(indices, extent):
    return (indices.astype(jnp.float32) - (extent - 1) / 2.0) * VELOCITY_STEP


def plane_speed(indices, extent):
    return CFL_NUMBER * (2 * indices - (extent - 1)).astype(jnp.float32) / (extent - 1)


def velocity_index(positions, extent):
    half = extent // 2
    return jnp.where(positions < half, positions, 3 * half - 1 - positions)


def tables(row_index, col_index, extent):
    phases = row_index[:, None] * col_index[None, :] % extent
    angles = phases.astype(jnp.float32) * (2.0 * math.pi / extent)
    return (jnp.cos(angles), jnp.sin(angles))


def multiply(table, operand):
    return jnp.einsum("ka,bam->bkm", table, operand, precision=lax.Precision.HIGHEST)


def rotate(operand, extent_mid, extent_low):
    batch_count, extent_top, merged = operand.shape
    shaped = operand.reshape(batch_count, extent_top, extent_mid, extent_low)
    return jnp.transpose(shaped, (0, 2, 3, 1)).reshape(
        batch_count, extent_mid, extent_low * extent_top
    )


def spectral(real_in, imag_in, orient, real_only):
    extents = (NVX, NVY, NVZ)
    real_now = real_in
    imag_now = imag_in
    for pass_index in range(3):
        extent = extents[pass_index]
        extent_mid = extents[(pass_index + 1) % 3]
        extent_low = extents[(pass_index + 2) % 3]
        plain = jnp.arange(extent, dtype=jnp.int32)
        if pass_index == 0 and orient < 0:
            cosines, sines = tables(plain, velocity_index(plain, extent), extent)
        elif pass_index == 0:
            cosines, sines = tables(velocity_index(plain, extent), plain, extent)
        else:
            cosines, sines = tables(plain, plain, extent)
        final_pass = real_only and pass_index == 2
        if imag_now is None:
            real_next = multiply(cosines, real_now)
            imag_next = orient * multiply(sines, real_now)
        else:
            real_next = multiply(cosines, real_now) - orient * multiply(sines, imag_now)
            if final_pass:
                imag_next = None
            else:
                imag_next = multiply(cosines, imag_now) + orient * multiply(sines, real_now)
        real_now = rotate(real_next, extent_mid, extent_low)
        imag_now = None if imag_next is None else rotate(imag_next, extent_mid, extent_low)
    return (real_now, imag_now)


def collide(heavy_block, fourier_scattering_table):
    species_count, x_extent_size, cell_count, merged = heavy_block.shape
    flattened = jnp.transpose(heavy_block, (0, 2, 1, 3)).reshape(
        species_count * cell_count, x_extent_size, merged
    )
    spec_real, spec_imag = spectral(flattened, None, -1, False)

    def invert(kernel_index):
        kernel = fourier_scattering_table[kernel_index][None, :, :]
        real_out, unused = spectral(spec_real * kernel, spec_imag * kernel, 1, True)
        return real_out / (NVX * NVY * NVZ)

    gain_sum = invert(0) * invert(1)
    loss_term = flattened * invert(2 * PAIRS)
    updated = flattened + COLLIDE_SCALE * (gain_sum - loss_term)
    return jnp.transpose(
        updated.reshape(species_count, cell_count, x_extent_size, merged), (0, 2, 1, 3)
    )


def split_bf16(values):
    rounded = lax.reduce_precision(values, exponent_bits=8, mantissa_bits=7)
    return rounded.astype(jnp.bfloat16), (values - rounded).astype(jnp.bfloat16)


def kron_tables(extent):
    size = extent * extent
    index = np.arange(size)
    phases = (
        np.outer(index // extent, index // extent) + np.outer(index % extent, index % extent)
    ) % extent
    angles = phases * (2.0 * np.pi / extent)

    def split(values):
        high = values.astype(jnp.bfloat16)
        low = (values - high.astype(np.float64)).astype(jnp.bfloat16)
        return jnp.asarray(high), jnp.asarray(low)

    return split(np.concatenate([np.cos(angles), np.sin(angles)], axis=1))


def split_dot(operand, table, table_dim=0):
    high, low = table
    op_high, op_low = split_bf16(operand)

    def dot(left, right):
        return lax.dot_general(
            left, right, (((1,), (table_dim,)), ((), ())), preferred_element_type=jnp.float32
        )

    return dot(op_high, high) + (dot(op_low, high) + dot(op_high, low))


def collide_kron(heavy_block, fourier_scattering_table):
    species_count, x_extent_size, cell_count, merged = heavy_block.shape
    hp = lax.Precision.HIGHEST
    flat = jnp.transpose(heavy_block, (0, 2, 1, 3)).reshape(
        species_count * cell_count, x_extent_size, merged
    )
    rows = species_count * cell_count
    kernel_count = fourier_scattering_table.shape[0]
    plain = jnp.arange(x_extent_size, dtype=jnp.int32)
    x_cos, x_sin = tables(plain, velocity_index(plain, x_extent_size), x_extent_size)
    wide = kron_tables(NVY)
    square = (x_extent_size, x_extent_size)
    forward = jnp.concatenate([x_cos, -x_sin], axis=0)
    spectrum_x = jnp.einsum(
        "bjp,bpm->bjm", jnp.broadcast_to(forward, (rows,) + forward.shape), flat, precision=hp
    )
    stacked = jnp.transpose(
        spectrum_x.reshape(rows, 2, x_extent_size, merged), (1, 0, 2, 3)
    ).reshape(-1, merged)
    both = split_dot(stacked, wide)
    by_cos = both[:, :merged].reshape(2, rows, x_extent_size, merged)
    by_sin = both[:, merged:].reshape(2, rows, x_extent_size, merged)
    spec_real = by_cos[0] + by_sin[1]
    spec_imag = by_cos[1] - by_sin[0]
    kernels = fourier_scattering_table[:, None]
    z_both = jnp.concatenate([kernels * spec_real[None], kernels * spec_imag[None]], axis=2)
    inverse = jnp.concatenate(
        [
            jnp.concatenate([x_cos.T, -x_sin.T], axis=1),
            jnp.concatenate([x_sin.T, x_cos.T], axis=1),
        ],
        axis=0,
    )
    u_both = jnp.einsum(
        "qbij,qbjm->qbim",
        jnp.broadcast_to(inverse, (kernel_count, rows) + inverse.shape),
        z_both,
        precision=hp,
    )
    u_real = u_both[:, :, :x_extent_size]
    u_imag = u_both[:, :, x_extent_size:]
    joined = jnp.concatenate([u_real, -u_imag], axis=3).reshape(-1, 2 * merged)
    parts = (
        split_dot(joined, wide, table_dim=1)
    ).reshape(kernel_count, rows, x_extent_size, merged) / (NVX * NVY * NVZ)
    updated = flat + COLLIDE_SCALE * (parts[0] * parts[1] - flat * parts[2])
    return jnp.transpose(
        updated.reshape(species_count, cell_count, x_extent_size, merged), (0, 2, 1, 3)
    )


def advance(padded, mirror, odd_stiffness_factor, leading_plane, x_extent_size):
    planes = padded.shape[1]
    positions = leading_plane + jnp.arange(planes, dtype=jnp.int32)
    speeds = plane_speed(velocity_index(positions, x_extent_size), x_extent_size)[
        None, :, None, None
    ]
    even_part = 0.5 * (padded + mirror)
    odd_part = 0.5 * (padded - mirror)
    even_diff = 0.5 * (even_part[:, :, 2:] - even_part[:, :, :-2])
    odd_diff = 0.5 * (odd_part[:, :, 2:] - odd_part[:, :, :-2])
    even_new = even_part[:, :, 1:-1] - speeds * odd_diff
    odd_new = (odd_part[:, :, 1:-1] - speeds * even_diff) / (1.0 + odd_stiffness_factor)[
        :, None, None, None
    ]
    return even_new + odd_new


def moments(light_portion, leading_plane, x_extent_size):
    planes = light_portion.shape[1]
    positions = leading_plane + jnp.arange(planes, dtype=jnp.int32)
    along_first = velocity_values(velocity_index(positions, x_extent_size), x_extent_size)
    along_second = jnp.repeat(velocity_values(jnp.arange(NVY, dtype=jnp.int32), NVY), NVZ)
    along_third = jnp.tile(velocity_values(jnp.arange(NVZ, dtype=jnp.int32), NVZ), NVY)
    density = jnp.sum(light_portion, axis=(1, 3))
    moment_first = jnp.sum(light_portion * along_first[None, :, None, None], axis=(1, 3))
    moment_second = jnp.sum(light_portion * along_second, axis=(1, 3))
    moment_third = jnp.sum(light_portion * along_third, axis=(1, 3))
    return jnp.stack([density, moment_first, moment_second, moment_third])


def relax_light_species(
    light_portion,
    summed_moments,
    leading_plane,
    x_extent_size,
    electron_bgk_frequency_dt,
    electron_kinetic_heat_level,
):
    light_count, planes, cell_count, merged = light_portion.shape
    density = summed_moments[0]
    drifts = summed_moments[1:] / density[None]
    equilibrium_heat_level = electron_kinetic_heat_level[:, None, None]

    def integration_coefficient(values, drift):
        offset_counts_per_row = values[None, None, :] - drift[:, :, None]
        return jnp.exp(
            -(offset_counts_per_row * offset_counts_per_row) / (2.0 * equilibrium_heat_level)
        )

    def profile(values, drift):
        weights = integration_coefficient(values, drift)
        return weights / jnp.sum(weights, axis=2, keepdims=True)

    full_first = integration_coefficient(
        velocity_values(jnp.arange(x_extent_size, dtype=jnp.int32), x_extent_size), drifts[0]
    )
    positions = leading_plane + jnp.arange(planes, dtype=jnp.int32)
    local_values = velocity_values(velocity_index(positions, x_extent_size), x_extent_size)
    local_first = integration_coefficient(local_values, drifts[0]) / jnp.sum(
        full_first, axis=2, keepdims=True
    )
    grid_second = velocity_values(jnp.arange(NVY, dtype=jnp.int32), NVY)
    grid_third = velocity_values(jnp.arange(NVZ, dtype=jnp.int32), NVZ)
    profile_rest = (
        profile(grid_second, drifts[1])[:, :, :, None]
        * profile(grid_third, drifts[2])[:, :, None, :]
    ).reshape(light_count, cell_count, merged)
    maxwell = (
        density[:, None, :, None]
        * jnp.transpose(local_first, (0, 2, 1))[:, :, :, None]
        * profile_rest[:, None, :, :]
    )
    rates = electron_bgk_frequency_dt[:, None, None, None]
    return (light_portion + rates * maxwell) / (1.0 + rates)


def body(
    phase_density_field,
    fourier_scattering_table,
    odd_stiffness_factor,
    electron_bgk_frequency_dt,
    electron_kinetic_heat_level,
):
    species_count = phase_density_field.shape[0]
    heavy_count = species_count - electron_bgk_frequency_dt.shape[0]
    x_extent_size = fourier_scattering_table.shape[1]
    planes = phase_density_field.shape[1]
    padded = extended(phase_density_field, (("space", 2),), 1)
    leading_plane = lax.axis_index("vel") * planes
    positions = leading_plane + jnp.arange(planes, dtype=jnp.int32)
    speeds = plane_speed(velocity_index(positions, x_extent_size), x_extent_size)[
        None, :, None, None
    ]
    shifted = phase_density_field - speeds * (
        0.5 * (padded[:, :, 2:] - padded[:, :, :-2])
    )
    gathered = lax.all_to_all(shifted, "vel", split_axis=2, concat_axis=1, tiled=True)
    half = x_extent_size // 2
    mirror = jnp.flip(
        jnp.concatenate([gathered[:, half:], gathered[:, :half]], axis=1), axis=3
    )
    ratio = 1.0 / (1.0 + odd_stiffness_factor)
    alpha = (0.5 * (1.0 + ratio))[:, None, None, None]
    beta = (0.5 * (1.0 - ratio))[:, None, None, None]
    advanced = alpha * gathered + beta * mirror
    heavy_part = collide_kron(advanced[:heavy_count], fourier_scattering_table)
    light_portion = advanced[heavy_count:]
    summed_moments = moments(light_portion, 0, x_extent_size)
    light_portion = relax_light_species(
        light_portion,
        summed_moments,
        0,
        x_extent_size,
        electron_bgk_frequency_dt,
        electron_kinetic_heat_level,
    )
    result = jnp.concatenate([heavy_part, light_portion], axis=0)
    return lax.all_to_all(result, "vel", split_axis=1, concat_axis=2, tiled=True)


def solution(mesh):
    in_specs = (P(None, "vel", "space", None), P(), P(), P(), P())
    out_specs = P(None, "vel", "space", None)
    return jax.shard_map(body, mesh=mesh, in_specs=in_specs, out_specs=out_specs, check_vma=False)
```

```python
import math

import numpy as np

import jax
import jax.numpy as jnp
from jax import lax
from jax.sharding import PartitionSpec as P

NVX = 32
NVY = 32
NVZ = 32
PAIRS = 1


CFL_NUMBER = 0.2
VELOCITY_STEP = 0.375
COLLIDE_SCALE = 0.25


def extended(x, sides, width):
    for axis, dim in sides:
        devices, length = (lax.axis_size(axis), x.shape[dim])
        up = [(i, (i + 1) % devices) for i in range(devices)]
        down = [(j, i) for i, j in up]
        last = lax.slice_in_dim(x, length - width, length, axis=dim)
        initial = lax.slice_in_dim(x, 0, width, axis=dim)
        before = lax.ppermute(last, axis, up)
        after = lax.ppermute(initial, axis, down)
        x = jnp.concatenate([before, x, after], axis=dim)
    return x


def from_partner(value, axis, stride):
    mask = 2**stride
    pairs = [(source, source ^ mask) for source in range(lax.axis_size(axis))]
    return lax.ppermute(value, axis, pairs)


def velocity_values(indices, extent):
    return (indices.astype(jnp.float32) - (extent - 1) / 2.0) * VELOCITY_STEP


def plane_speed(indices, extent):
    return CFL_NUMBER * (2 * indices - (extent - 1)).astype(jnp.float32) / (extent - 1)


def velocity_index(positions, extent):
    half = extent // 2
    return jnp.where(positions < half, positions, 3 * half - 1 - positions)


def tables(row_index, col_index, extent):
    phases = row_index[:, None] * col_index[None, :] % extent
    angles = phases.astype(jnp.float32) * (2.0 * math.pi / extent)
    return (jnp.cos(angles), jnp.sin(angles))


def multiply(table, operand):
    return jnp.einsum("ka,bam->bkm", table, operand, precision=lax.Precision.HIGHEST)


def rotate(operand, extent_mid, extent_low):
    batch_count, extent_top, merged = operand.shape
    shaped = operand.reshape(batch_count, extent_top, extent_mid, extent_low)
    return jnp.transpose(shaped, (0, 2, 3, 1)).reshape(
        batch_count, extent_mid, extent_low * extent_top
    )


def spectral(real_in, imag_in, orient, real_only):
    extents = (NVX, NVY, NVZ)
    real_now = real_in
    imag_now = imag_in
    for pass_index in range(3):
        extent = extents[pass_index]
        extent_mid = extents[(pass_index + 1) % 3]
        extent_low = extents[(pass_index + 2) % 3]
        plain = jnp.arange(extent, dtype=jnp.int32)
        if pass_index == 0 and orient < 0:
            cosines, sines = tables(plain, velocity_index(plain, extent), extent)
        elif pass_index == 0:
            cosines, sines = tables(velocity_index(plain, extent), plain, extent)
        else:
            cosines, sines = tables(plain, plain, extent)
        final_pass = real_only and pass_index == 2
        if imag_now is None:
            real_next = multiply(cosines, real_now)
            imag_next = orient * multiply(sines, real_now)
        else:
            real_next = multiply(cosines, real_now) - orient * multiply(sines, imag_now)
            if final_pass:
                imag_next = None
            else:
                imag_next = multiply(cosines, imag_now) + orient * multiply(sines, real_now)
        real_now = rotate(real_next, extent_mid, extent_low)
        imag_now = None if imag_next is None else rotate(imag_next, extent_mid, extent_low)
    return (real_now, imag_now)


def collide(heavy_block, fourier_scattering_table):
    species_count, x_extent_size, cell_count, merged = heavy_block.shape
    flattened = jnp.transpose(heavy_block, (0, 2, 1, 3)).reshape(
        species_count * cell_count, x_extent_size, merged
    )
    spec_real, spec_imag = spectral(flattened, None, -1, False)

    def invert(kernel_index):
        kernel = fourier_scattering_table[kernel_index][None, :, :]
        real_out, unused = spectral(spec_real * kernel, spec_imag * kernel, 1, True)
        return real_out / (NVX * NVY * NVZ)

    gain_sum = invert(0) * invert(1)
    loss_term = flattened * invert(2 * PAIRS)
    updated = flattened + COLLIDE_SCALE * (gain_sum - loss_term)
    return jnp.transpose(
        updated.reshape(species_count, cell_count, x_extent_size, merged), (0, 2, 1, 3)
    )


def split_bf16(values):
    rounded = lax.reduce_precision(values, exponent_bits=8, mantissa_bits=7)
    return rounded.astype(jnp.bfloat16), (values - rounded).astype(jnp.bfloat16)


def kron_tables(extent):
    size = extent * extent
    index = np.arange(size)
    phases = (
        np.outer(index // extent, index // extent) + np.outer(index % extent, index % extent)
    ) % extent
    angles = phases * (2.0 * np.pi / extent)

    def split(values):
        high = values.astype(jnp.bfloat16)
        low = (values - high.astype(np.float64)).astype(jnp.bfloat16)
        return jnp.asarray(high), jnp.asarray(low)

    return split(np.concatenate([np.cos(angles), np.sin(angles)], axis=1))


def split_dot(operand, table, table_dim=0):
    high, low = table
    op_high, op_low = split_bf16(operand)

    def dot(left, right):
        return lax.dot_general(
            left, right, (((1,), (table_dim,)), ((), ())), preferred_element_type=jnp.float32
        )

    return dot(op_high, high) + (dot(op_low, high) + dot(op_high, low))


def collide_kron(heavy_block, fourier_scattering_table):
    species_count, x_extent_size, cell_count, merged = heavy_block.shape
    hp = lax.Precision.HIGH
    flat = jnp.transpose(heavy_block, (0, 2, 1, 3)).reshape(
        species_count * cell_count, x_extent_size, merged
    )
    rows = species_count * cell_count
    kernel_count = fourier_scattering_table.shape[0]
    plain = jnp.arange(x_extent_size, dtype=jnp.int32)
    x_cos, x_sin = tables(plain, velocity_index(plain, x_extent_size), x_extent_size)
    wide = kron_tables(NVY)
    square = (x_extent_size, x_extent_size)
    forward = jnp.concatenate([x_cos, -x_sin], axis=0)
    spectrum_x = jnp.einsum(
        "bjp,bpm->bjm", jnp.broadcast_to(forward, (rows,) + forward.shape), flat, precision=hp
    )
    stacked = jnp.transpose(
        spectrum_x.reshape(rows, 2, x_extent_size, merged), (1, 0, 2, 3)
    ).reshape(-1, merged)
    both = split_dot(stacked, wide)
    by_cos = both[:, :merged].reshape(2, rows, x_extent_size, merged)
    by_sin = both[:, merged:].reshape(2, rows, x_extent_size, merged)
    spec_real = by_cos[0] + by_sin[1]
    spec_imag = by_cos[1] - by_sin[0]
    kernels = fourier_scattering_table[:, None]
    z_both = jnp.concatenate([kernels * spec_real[None], kernels * spec_imag[None]], axis=2)
    inverse = jnp.concatenate(
        [
            jnp.concatenate([x_cos.T, -x_sin.T], axis=1),
            jnp.concatenate([x_sin.T, x_cos.T], axis=1),
        ],
        axis=0,
    )
    u_both = jnp.einsum(
        "qbij,qbjm->qbim",
        jnp.broadcast_to(inverse, (kernel_count, rows) + inverse.shape),
        z_both,
        precision=hp,
    )
    u_real = u_both[:, :, :x_extent_size]
    u_imag = u_both[:, :, x_extent_size:]
    joined = jnp.concatenate([u_real, -u_imag], axis=3).reshape(-1, 2 * merged)
    parts = (
        split_dot(joined, wide, table_dim=1)
    ).reshape(kernel_count, rows, x_extent_size, merged) / (NVX * NVY * NVZ)
    updated = flat + COLLIDE_SCALE * (parts[0] * parts[1] - flat * parts[2])
    return jnp.transpose(
        updated.reshape(species_count, cell_count, x_extent_size, merged), (0, 2, 1, 3)
    )


def advance(padded, mirror, odd_stiffness_factor, leading_plane, x_extent_size):
    planes = padded.shape[1]
    positions = leading_plane + jnp.arange(planes, dtype=jnp.int32)
    speeds = plane_speed(velocity_index(positions, x_extent_size), x_extent_size)[
        None, :, None, None
    ]
    even_part = 0.5 * (padded + mirror)
    odd_part = 0.5 * (padded - mirror)
    even_diff = 0.5 * (even_part[:, :, 2:] - even_part[:, :, :-2])
    odd_diff = 0.5 * (odd_part[:, :, 2:] - odd_part[:, :, :-2])
    even_new = even_part[:, :, 1:-1] - speeds * odd_diff
    odd_new = (odd_part[:, :, 1:-1] - speeds * even_diff) / (1.0 + odd_stiffness_factor)[
        :, None, None, None
    ]
    return even_new + odd_new


def moments(light_portion, leading_plane, x_extent_size):
    planes = light_portion.shape[1]
    positions = leading_plane + jnp.arange(planes, dtype=jnp.int32)
    along_first = velocity_values(velocity_index(positions, x_extent_size), x_extent_size)
    along_second = jnp.repeat(velocity_values(jnp.arange(NVY, dtype=jnp.int32), NVY), NVZ)
    along_third = jnp.tile(velocity_values(jnp.arange(NVZ, dtype=jnp.int32), NVZ), NVY)
    density = jnp.sum(light_portion, axis=(1, 3))
    moment_first = jnp.sum(light_portion * along_first[None, :, None, None], axis=(1, 3))
    moment_second = jnp.sum(light_portion * along_second, axis=(1, 3))
    moment_third = jnp.sum(light_portion * along_third, axis=(1, 3))
    return jnp.stack([density, moment_first, moment_second, moment_third])


def relax_light_species(
    light_portion,
    summed_moments,
    leading_plane,
    x_extent_size,
    electron_bgk_frequency_dt,
    electron_kinetic_heat_level,
):
    light_count, planes, cell_count, merged = light_portion.shape
    density = summed_moments[0]
    drifts = summed_moments[1:] / density[None]
    equilibrium_heat_level = electron_kinetic_heat_level[:, None, None]

    def integration_coefficient(values, drift):
        offset_counts_per_row = values[None, None, :] - drift[:, :, None]
        return jnp.exp(
            -(offset_counts_per_row * offset_counts_per_row) / (2.0 * equilibrium_heat_level)
        )

    def profile(values, drift):
        weights = integration_coefficient(values, drift)
        return weights / jnp.sum(weights, axis=2, keepdims=True)

    full_first = integration_coefficient(
        velocity_values(jnp.arange(x_extent_size, dtype=jnp.int32), x_extent_size), drifts[0]
    )
    positions = leading_plane + jnp.arange(planes, dtype=jnp.int32)
    local_values = velocity_values(velocity_index(positions, x_extent_size), x_extent_size)
    local_first = integration_coefficient(local_values, drifts[0]) / jnp.sum(
        full_first, axis=2, keepdims=True
    )
    grid_second = velocity_values(jnp.arange(NVY, dtype=jnp.int32), NVY)
    grid_third = velocity_values(jnp.arange(NVZ, dtype=jnp.int32), NVZ)
    profile_rest = (
        profile(grid_second, drifts[1])[:, :, :, None]
        * profile(grid_third, drifts[2])[:, :, None, :]
    ).reshape(light_count, cell_count, merged)
    maxwell = (
        density[:, None, :, None]
        * jnp.transpose(local_first, (0, 2, 1))[:, :, :, None]
        * profile_rest[:, None, :, :]
    )
    rates = electron_bgk_frequency_dt[:, None, None, None]
    return (light_portion + rates * maxwell) / (1.0 + rates)


def body(
    phase_density_field,
    fourier_scattering_table,
    odd_stiffness_factor,
    electron_bgk_frequency_dt,
    electron_kinetic_heat_level,
):
    species_count = phase_density_field.shape[0]
    heavy_count = species_count - electron_bgk_frequency_dt.shape[0]
    x_extent_size = fourier_scattering_table.shape[1]
    planes = phase_density_field.shape[1]
    padded = extended(phase_density_field, (("space", 2),), 1)
    leading_plane = lax.axis_index("vel") * planes
    positions = leading_plane + jnp.arange(planes, dtype=jnp.int32)
    speeds = plane_speed(velocity_index(positions, x_extent_size), x_extent_size)[
        None, :, None, None
    ]
    shifted = phase_density_field - speeds * (
        0.5 * (padded[:, :, 2:] - padded[:, :, :-2])
    )
    gathered = lax.all_to_all(shifted, "vel", split_axis=2, concat_axis=1, tiled=True)
    half = x_extent_size // 2
    mirror = jnp.flip(
        jnp.concatenate([gathered[:, half:], gathered[:, :half]], axis=1), axis=3
    )
    ratio = 1.0 / (1.0 + odd_stiffness_factor)
    alpha = (0.5 * (1.0 + ratio))[:, None, None, None]
    beta = (0.5 * (1.0 - ratio))[:, None, None, None]
    advanced = alpha * gathered + beta * mirror
    heavy_part = collide_kron(advanced[:heavy_count], fourier_scattering_table)
    light_portion = advanced[heavy_count:]
    summed_moments = moments(light_portion, 0, x_extent_size)
    light_portion = relax_light_species(
        light_portion,
        summed_moments,
        0,
        x_extent_size,
        electron_bgk_frequency_dt,
        electron_kinetic_heat_level,
    )
    result = jnp.concatenate([heavy_part, light_portion], axis=0)
    return lax.all_to_all(result, "vel", split_axis=1, concat_axis=2, tiled=True)


def solution(mesh):
    in_specs = (P(None, "vel", "space", None), P(), P(), P(), P())
    out_specs = P(None, "vel", "space", None)
    return jax.shard_map(body, mesh=mesh, in_specs=in_specs, out_specs=out_specs, check_vma=False)
```
